256 devices in a mesh: ment: 64 (over z, x, core), ent: 4 (over y).
Axes of the slice: x: 4, y: 4, z: 8, core: 2. Of those that a mesh axis runs over, the one named last changes fastest.
Arguments:
- hidden_in: bfloat16 [4096, 32, 1024], P('ment'), may hold values from -16 to 16
- w_qkv: bfloat16 [1024, 3, 1024], P(None, None, 'ent'), may hold values from -0.1875 to 0.1875
- w_out: bfloat16 [1024, 1024], P('ent'), may hold values from -0.1875 to 0.1875
- ln_gain: float32 [1024], replicated, may hold values from 0.5 to 1.5
- ln_bias: float32 [1024], replicated, may hold values from -3 to 3
- table: bfloat16 [32, 256, 1024], P('ent'), may hold values from -0.5 to 0.5
- key_len: int32 [4096], P('ment'), may hold values from 4 to 32
- gold_block: int32 [4096], P('ment'), may hold values from 0 to 31
- gold_row: int32 [4096], P('ment'), may hold values from 0 to 255
- neg_blocks: int32 [64, 4], P('ment'), may hold values from 0 to 31, as said below
Outputs:
- grad_hidden: bfloat16 [4096, 32, 1024], P(('ment', 'ent'))
- grad_qkv: float32 [1024, 3, 1024], P('ment', None, 'ent')
- grad_wo: float32 [1024, 1024], P('ent', 'ment')
- grad_ln: float32 [2, 1024], P(None, 'ment')
- grad_table: float32 [32, 256, 1024], P('ent', 'ment')
The draws below stay inside these ranges and needn't reach their ends.
Inputs may be any that keep to these rules, and one draw needn't show every extreme that they name: `neg_blocks`: each row lists 4 different blocks.
All inputs are finite; a program needn't handle non-finite values.
Results may differ from the reference program's by a relative error of at most 0.028.
Values may be sent and summed in bfloat16 or wider, within the bound.
A program may use at most 128 MiB of HBM per device.

```python
import jax
import jax.numpy as jnp
from jax import lax

MODEL_WIDTH = 1024
HEADS = 16
HD = 64
L = 32
MB = 64
BLK = 256
NEGB = 4
REPLICAS = 64
MENTIONS = 4096
NBLK = 32


def draw_neg_blocks(key, part):
    base = jax.random.randint(key, (REPLICAS, NBLK), 0, 65536)
    heat = jax.random.randint(jax.random.fold_in(key, 7), (NBLK,), 0, 4)
    top_owner = jax.random.randint(jax.random.fold_in(key, 11), (), 0, REPLICAS)
    low_owner = jax.random.randint(jax.random.fold_in(key, 13), (), 0, REPLICAS)
    boost = jnp.zeros((REPLICAS, NBLK), jnp.int32)
    boost = boost.at[top_owner, NBLK - 1].set(4)
    boost = boost.at[low_owner, 0].set(4)
    ranked = (base + (heat[None, :] + boost) * 65536) * NBLK + jnp.arange(NBLK, dtype=jnp.int32)[None, :]
    picked = lax.top_k(ranked, NEGB)[1]
    return picked.astype(jnp.int32)


def with_ends(entries, stream_key, least, top_value):
    spot = [jax.random.randint(jax.random.fold_in(stream_key, axis), (), 0, length) for axis, length in enumerate(entries.shape)]
    longest = entries.shape.index(max(entries.shape))
    neighbour = spot[:longest] + [(spot[longest] + 1) % entries.shape[longest]] + spot[longest + 1:]
    return entries.at[tuple(spot)].set(least).at[tuple(neighbour)].set(top_value)


def with_spikes(array, rng, source, target, shards_of, factor):
    def block_of(axis_at):
        return (jnp.arange(array.shape[axis_at]) // (array.shape[axis_at] // shards_of)).reshape((-1,) + (1,) * (array.ndim - 1 - axis_at))

    one_side = jax.random.permutation(rng, shards_of)[block_of(target)]
    other_side = (block_of(target) + shards_of // 2) % shards_of
    return jnp.where((block_of(source) == one_side) | (block_of(source) == other_side), factor * array, array)


def block_levels(key, extent, shards, low, largest):
    gain = 1.0
    for position, parts in shards:
        steps = jax.random.uniform(jax.random.fold_in(jax.random.fold_in(key, 6), position), (parts,), jnp.float32, low / len(shards), largest / len(shards))
        gain = gain * jnp.repeat(jnp.exp(steps), extent[position] // parts).reshape((-1,) + (1,) * (len(extent) - 1 - position))
    return gain


def gaussian(key, shape, deviation, bound, pieces=(), kind=jnp.bfloat16):
    level = block_levels(key, shape, pieces, -0.22, 0.18) if pieces else 1.0
    entries = jax.random.normal(key, shape, jnp.float32) * deviation * level
    return jnp.minimum(jnp.maximum(entries, -bound), bound).astype(kind)


def gaussian_with(key, extent, spread, reach, pieces, heavy, kind=jnp.bfloat16):
    array = spread * jax.random.normal(key, extent, jnp.float32)
    if pieces:
        array = array * block_levels(key, extent, pieces, -0.22, 0.18)
    return jnp.clip(with_spikes(array, jax.random.fold_in(key, 3), *heavy), -reach, reach).astype(kind)


def setup_inputs(seed: int = 0) -> dict:
    splits = jax.random.split(jax.random.key(seed), 11)
    return {
        "hidden_in": gaussian_with(splits[0], (MENTIONS, L, MODEL_WIDTH), 1.0, 16.0, ((0, 64),), (0, 2, 64, 4.0)),
        "w_qkv": gaussian(splits[1], (MODEL_WIDTH, 3, MODEL_WIDTH), MODEL_WIDTH ** -0.5, 0.1875, ((2, 4),)),
        "w_out": gaussian(splits[2], (MODEL_WIDTH, MODEL_WIDTH), MODEL_WIDTH ** -0.5, 0.1875, ((0, 4),)),
        "ln_gain": jnp.clip(1.0 + 0.1 * jax.random.normal(splits[3], (MODEL_WIDTH,), jnp.float32), 0.5, 1.5),
        "ln_bias": gaussian(splits[4], (MODEL_WIDTH,), 0.5, 3.0, (), jnp.float32),
        "table": gaussian(splits[5], (NBLK, BLK, MODEL_WIDTH), (MODEL_WIDTH // 9) ** -0.5, 0.5, ((0, 4),)),
        "key_len": with_ends(jax.random.randint(splits[6], (MENTIONS,), 4, L + 1), jax.random.fold_in(splits[6], 1), 4, L).astype(jnp.int32),
        "gold_block": with_ends(jax.random.randint(splits[7], (MENTIONS,), 0, NBLK), jax.random.fold_in(splits[7], 1), 0, NBLK - 1).astype(jnp.int32),
        "gold_row": with_ends(jax.random.randint(splits[8], (MENTIONS,), 0, BLK), jax.random.fold_in(splits[8], 1), 0, BLK - 1).astype(jnp.int32),
        "neg_blocks": draw_neg_blocks(jax.random.fold_in(splits[10], 71), 0),
    }


ln_eps = 1e-06

def reference(hidden_in, w_qkv, w_out, ln_gain, ln_bias, table, key_len, gold_block, gold_row, neg_blocks):
    gradient_total = hidden_in.shape[0]
    score_scale = HD ** (-0.5)
    cls_rows = hidden_in[:, 0, :]
    query = jnp.dot(cls_rows, w_qkv[:, 0, :], preferred_element_type=jnp.float32).astype(jnp.bfloat16)
    w_keyval = w_qkv[:, 1:, :].reshape(MODEL_WIDTH, 2 * MODEL_WIDTH)
    keyval = jnp.dot(hidden_in.reshape(gradient_total * L, MODEL_WIDTH), w_keyval, preferred_element_type=jnp.float32)
    keyval = keyval.astype(jnp.bfloat16).reshape(gradient_total, L, 2, HEADS, HD)
    key_heads = keyval[:, :, 0].astype(jnp.float32)
    value_heads = keyval[:, :, 1].astype(jnp.float32)
    query_heads = query.reshape(gradient_total, HEADS, HD).astype(jnp.float32)
    attention_scores = jnp.einsum('ybn,yqbn->ybq', query_heads, key_heads) * score_scale
    valid = (jnp.arange(L, dtype=jnp.int32)[None, :] < key_len[:, None]).astype(jnp.float32)
    expo = jnp.exp(attention_scores) * valid[:, None, :]
    probs = expo / lax.optimization_barrier(jnp.sum(expo, axis=-1, keepdims=True))
    probability_half = probs.astype(jnp.bfloat16)
    context_rows = jnp.einsum('qjp,qpjb->qjb', probability_half.astype(jnp.float32), value_heads)
    context_rows = context_rows.reshape(gradient_total, MODEL_WIDTH).astype(jnp.bfloat16)
    resid = cls_rows.astype(jnp.float32) + jnp.dot(context_rows, w_out, preferred_element_type=jnp.float32)
    centre = resid - lax.optimization_barrier(jnp.mean(resid, axis=-1, keepdims=True))
    rstd = lax.rsqrt(lax.optimization_barrier(jnp.mean(centre * centre, axis=-1, keepdims=True)) + ln_eps)
    normed = centre * rstd
    embed = (normed * ln_gain + ln_bias).astype(jnp.bfloat16)
    flat_table = table.reshape(NBLK * BLK, MODEL_WIDTH)
    gold_index = (gold_block * BLK + gold_row).astype(jnp.int32)
    golds = flat_table[gold_index]
    embed_r = embed.reshape(REPLICAS, MB, MODEL_WIDTH).astype(jnp.float32)
    golds_r = golds.reshape(REPLICAS, MB, MODEL_WIDTH).astype(jnp.float32)
    inbatch = jnp.einsum('rmd,rnd->rmn', embed_r, golds_r)
    negscore = jnp.dot(embed, flat_table.T, preferred_element_type=jnp.float32)
    listed = jnp.any(neg_blocks[:, :, None] == jnp.arange(NBLK, dtype=jnp.int32)[None, None, :], axis=1)
    listed = jnp.repeat(listed.astype(jnp.float32), MB, axis=0)
    row_mask = jnp.repeat(listed, BLK, axis=1)
    norm_total = lax.optimization_barrier(jnp.sum(jnp.exp(inbatch), axis=-1)).reshape(gradient_total) + lax.optimization_barrier(jnp.sum(jnp.exp(negscore) * row_mask, axis=-1))
    lse = jnp.log(norm_total)
    eye = jnp.eye(MB, dtype=jnp.float32)
    w_inb = (jnp.exp(inbatch - lse.reshape(REPLICAS, MB, 1)) - eye[None]).astype(jnp.bfloat16)
    w_neg = (jnp.exp(negscore - lse[:, None]) * row_mask).astype(jnp.bfloat16)
    d_embed = jnp.einsum('rmn,rnd->rmd', w_inb.astype(jnp.float32), golds_r).reshape(gradient_total, MODEL_WIDTH)
    d_embed = d_embed + jnp.dot(w_neg, flat_table, preferred_element_type=jnp.float32)
    gold_terms = jnp.einsum('rmn,rmd->rnd', w_inb.astype(jnp.float32), embed_r).reshape(gradient_total, MODEL_WIDTH)
    grad_table = jnp.dot(w_neg.T, embed, preferred_element_type=jnp.float32)
    grad_table = grad_table.at[gold_index].add(gold_terms)
    grad_ln = jnp.stack([lax.optimization_barrier(jnp.sum(d_embed * normed, axis=0)), lax.optimization_barrier(jnp.sum(d_embed, axis=0))])
    upper = d_embed * ln_gain
    d_resid = rstd * (upper - lax.optimization_barrier(jnp.mean(upper, axis=-1, keepdims=True)) - normed * lax.optimization_barrier(jnp.mean(upper * normed, axis=-1, keepdims=True)))
    d_resid_bf = d_resid.astype(jnp.bfloat16)
    grad_wo = jnp.dot(context_rows.T, d_resid_bf, preferred_element_type=jnp.float32)
    d_context = jnp.dot(d_resid_bf, w_out.T, preferred_element_type=jnp.float32).astype(jnp.bfloat16)
    context_head_gradient = d_context.reshape(gradient_total, HEADS, HD).astype(jnp.float32)
    probability_gradient = jnp.einsum('ybn,yqbn->ybq', context_head_gradient, value_heads)
    score_gradient = probs * (probability_gradient - lax.optimization_barrier(jnp.sum(probs * probability_gradient, axis=-1, keepdims=True)))
    query_gradient = (jnp.einsum('qjp,qpjb->qjb', score_gradient, key_heads) * score_scale).reshape(gradient_total, MODEL_WIDTH).astype(jnp.bfloat16)
    key_gradient = jnp.einsum('ryk,ryo->rkyo', score_gradient, query_heads) * score_scale
    value_gradient = jnp.einsum('ryk,ryo->rkyo', probability_half.astype(jnp.float32), context_head_gradient)
    d_keyval = jnp.stack([key_gradient, value_gradient], axis=2).reshape(gradient_total * L, 2 * MODEL_WIDTH).astype(jnp.bfloat16)
    grad_query = jnp.dot(cls_rows.T, query_gradient, preferred_element_type=jnp.float32)
    grad_keyval = jnp.dot(hidden_in.reshape(gradient_total * L, MODEL_WIDTH).T, d_keyval, preferred_element_type=jnp.float32)
    grad_qkv = jnp.concatenate([grad_query[:, None, :], grad_keyval.reshape(MODEL_WIDTH, 2, MODEL_WIDTH)], axis=1)
    input_grad = jnp.dot(d_keyval, w_keyval.T, preferred_element_type=jnp.float32).reshape(gradient_total, L, MODEL_WIDTH)
    cls_grad = jnp.dot(query_gradient, w_qkv[:, 0, :].T, preferred_element_type=jnp.float32) + d_resid
    input_grad = input_grad.at[:, 0, :].add(cls_grad)
    return (input_grad.astype(jnp.bfloat16), grad_qkv, grad_wo, grad_ln, grad_table.reshape(NBLK, BLK, MODEL_WIDTH))
```

```python
import jax
import jax.numpy as jnp
from jax import lax
from jax.sharding import PartitionSpec as P

HD = 64


ln_eps = 1e-06


def contract(left, right, left_dim, right_dim):
    return lax.dot_general(
        left, right, (((left_dim,), (right_dim,)), ((), ())), preferred_element_type=jnp.float32
    )


def on_device(
    hidden_in, w_qkv, w_out, ln_gain, ln_bias, table, key_len, gold_block, gold_row, neg_blocks
):
    ment_rows, seq_len, width = hidden_in.shape
    local_cols = w_qkv.shape[2]
    local_heads = local_cols // HD
    own_blocks, block_rows = (table.shape[0], table.shape[1])
    score_scale = HD ** (-0.5)
    owner = lax.axis_index("ent")
    first_block = owner * own_blocks
    cls_rows = hidden_in[:, 0, :]
    w_query = w_qkv[:, 0, :]
    w_keyval = w_qkv[:, 1:, :].reshape(width, 2 * local_cols)
    query = jnp.dot(cls_rows, w_query, preferred_element_type=jnp.float32).astype(jnp.bfloat16)
    keyval = jnp.dot(
        hidden_in.reshape(ment_rows * seq_len, width), w_keyval, preferred_element_type=jnp.float32
    )
    keyval = keyval.astype(jnp.bfloat16).reshape(ment_rows, seq_len, 2, local_heads, HD)
    key_heads = keyval[:, :, 0]
    value_heads = keyval[:, :, 1]
    query_heads = query.reshape(ment_rows, local_heads, HD)
    attention_scores = (
        jnp.einsum("ybn,yqbn->ybq", query_heads, key_heads, preferred_element_type=jnp.float32)
        * score_scale
    )
    valid = (jnp.arange(seq_len, dtype=jnp.int32)[None, :] < key_len[:, None]).astype(jnp.float32)
    expo = jnp.exp(attention_scores) * valid[:, None, :]
    probs = expo / jnp.sum(expo, axis=-1, keepdims=True)
    probability_half = probs.astype(jnp.bfloat16)
    context_rows = jnp.einsum(
        "qjp,qpjb->qjb", probability_half, value_heads, preferred_element_type=jnp.float32
    )
    context_rows = context_rows.reshape(ment_rows, local_cols).astype(jnp.bfloat16)
    attn_part = jnp.dot(context_rows, w_out, preferred_element_type=jnp.float32)
    local_block = gold_block - first_block
    owned = (local_block >= 0) & (local_block < own_blocks)
    safe_block = jnp.clip(local_block, 0, own_blocks - 1)
    flat_table = table.reshape(own_blocks * block_rows, width)
    picked = flat_table[safe_block * block_rows + gold_row]
    picked = jnp.where(owned[:, None], picked.astype(jnp.float32), 0.0)
    attn_out, gold_sum = (
        lax.psum(attn_part.astype(jnp.bfloat16), "ent").astype(jnp.float32),
        lax.psum(picked.astype(jnp.bfloat16), "ent").astype(jnp.float32),
    )
    golds = gold_sum.astype(jnp.bfloat16)
    resid = cls_rows.astype(jnp.float32) + attn_out
    centre = resid - jnp.mean(resid, axis=-1, keepdims=True)
    rstd = lax.rsqrt(jnp.mean(centre * centre, axis=-1, keepdims=True) + ln_eps)
    normed = centre * rstd
    embed = (normed * ln_gain + ln_bias).astype(jnp.bfloat16)
    inbatch = contract(embed, golds, 1, 1)
    negscore = contract(embed, flat_table, 1, 1)
    block_ids = first_block + jnp.arange(own_blocks, dtype=jnp.int32)
    listed = jnp.any(neg_blocks[0][:, None] == block_ids[None, :], axis=0).astype(jnp.float32)
    row_mask = jnp.repeat(listed, block_rows)
    neg_part = jnp.sum(jnp.exp(negscore) * row_mask[None, :], axis=1)
    neg_total = lax.psum(neg_part, "ent")
    lse = jnp.log(jnp.sum(jnp.exp(inbatch), axis=1) + neg_total)
    eye = jnp.eye(ment_rows, dtype=jnp.float32)
    w_inb = (jnp.exp(inbatch - lse[:, None]) - eye).astype(jnp.bfloat16)
    w_neg = (jnp.exp(negscore - lse[:, None]) * row_mask[None, :]).astype(jnp.bfloat16)
    embed_part = jnp.dot(w_neg, flat_table, preferred_element_type=jnp.float32)
    d_embed = jnp.dot(w_inb, golds, preferred_element_type=jnp.float32) + lax.psum(
        embed_part.astype(jnp.bfloat16), "ent"
    ).astype(jnp.float32)
    ln_terms = jnp.stack([jnp.sum(d_embed * normed, axis=0), jnp.sum(d_embed, axis=0)])
    upper = d_embed * ln_gain
    d_resid = rstd * (
        upper
        - jnp.mean(upper, axis=-1, keepdims=True)
        - normed * jnp.mean(upper * normed, axis=-1, keepdims=True)
    )
    d_resid_bf = d_resid.astype(jnp.bfloat16)
    wo_term = contract(context_rows, d_resid_bf, 0, 0)
    d_context = contract(d_resid_bf, w_out, 1, 1).astype(jnp.bfloat16)
    context_head_gradient = d_context.reshape(ment_rows, local_heads, HD)
    probability_gradient = jnp.einsum(
        "ybn,yqbn->ybq", context_head_gradient, value_heads, preferred_element_type=jnp.float32
    )
    score_gradient = probs * (
        probability_gradient - jnp.sum(probs * probability_gradient, axis=-1, keepdims=True)
    )
    query_gradient = (
        jnp.einsum("qjp,qpjb->qjb", score_gradient, key_heads, preferred_element_type=jnp.float32)
        * score_scale
    )
    query_gradient = query_gradient.reshape(ment_rows, local_cols).astype(jnp.bfloat16)
    key_gradient = (
        jnp.einsum("ryk,ryo->rkyo", score_gradient, query_heads, preferred_element_type=jnp.float32)
        * score_scale
    )
    value_gradient = jnp.einsum(
        "ryk,ryo->rkyo", probability_half, context_head_gradient, preferred_element_type=jnp.float32
    )
    d_keyval = (
        jnp.stack([key_gradient, value_gradient], axis=2)
        .reshape(ment_rows, seq_len, 2 * local_cols)
        .astype(jnp.bfloat16)
    )
    flat_grad = d_keyval.reshape(ment_rows * seq_len, 2 * local_cols)
    count = lax.axis_size("ment") * (width // lax.axis_size("ment"))
    kv_term = contract(hidden_in.reshape(ment_rows * seq_len, count), flat_grad, 0, 0)
    query_term = contract(hidden_in[:, 0, :], query_gradient, 0, 0)
    qkv_term = jnp.concatenate(
        [query_term[:, None, :], kv_term.reshape(count, 2, local_cols)], axis=1
    )
    share = ment_rows // lax.axis_size("ent")
    grad_part = d_keyval.reshape(share * lax.axis_size("ent") * seq_len, 2 * local_cols)
    token_term = contract(grad_part, w_keyval, 1, 1).reshape(
        share * lax.axis_size("ent"), seq_len, width
    )
    summed = lax.psum_scatter(
        token_term.at[:, 0, :].add(contract(query_gradient, w_query, 1, 1)).astype(jnp.bfloat16),
        "ent",
        scatter_dimension=0,
        tiled=True,
    ).astype(jnp.float32)
    resid_mine = lax.dynamic_slice_in_dim(d_resid, owner * share, share, 0)
    grad_hidden = summed.at[:, 0, :].add(resid_mine).astype(jnp.bfloat16)
    gold_terms = contract(w_inb, embed, 0, 0)
    weight_blocks = w_neg.reshape(ment_rows, own_blocks, block_rows)
    count = lax.axis_size("ment") * (block_rows // lax.axis_size("ment"))
    neg_term = jnp.einsum("mbr,md->rbd", weight_blocks, embed, preferred_element_type=jnp.float32)
    inside = owned & (gold_row >= 0) & (gold_row < count)
    row_slot = jnp.where(inside, gold_row, count)
    table_term = neg_term.at[row_slot, safe_block].add(gold_terms, mode="drop")
    parts = lax.axis_size("ment")
    qkv_rows = width // parts
    wo_cols = width // parts
    tab_rows = block_rows // parts
    pieces = [
        qkv_term.reshape(parts, qkv_rows * 3 * local_cols),
        wo_term.reshape(local_cols, parts, wo_cols).transpose(1, 0, 2).reshape(parts, -1),
        table_term.reshape(parts, tab_rows, own_blocks, width)
        .transpose(0, 2, 1, 3)
        .reshape(parts, -1),
        ln_terms.reshape(2, parts, wo_cols).transpose(1, 0, 2).reshape(parts, -1),
    ]
    sizes = [piece.shape[1] for piece in pieces]
    padded = -sum(sizes) % 1024
    pieces.append(jnp.zeros((parts, padded), jnp.float32))
    stacked = jnp.concatenate(pieces, axis=1).reshape(parts * 8, -1)
    merged = lax.psum_scatter(stacked, "ment", scatter_dimension=0, tiled=True).reshape(-1)
    offsets = [sum(sizes[:k]) for k in range(len(sizes))]
    grad_qkv = merged[offsets[0] : offsets[0] + sizes[0]].reshape(qkv_rows, 3, local_cols)
    grad_wo = merged[offsets[1] : offsets[1] + sizes[1]].reshape(local_cols, wo_cols)
    grad_table = merged[offsets[2] : offsets[2] + sizes[2]].reshape(own_blocks, tab_rows, width)
    grad_ln = merged[offsets[3] : offsets[3] + sizes[3]].reshape(2, wo_cols)
    return (grad_hidden, grad_qkv, grad_wo, grad_ln, grad_table)


def solution(mesh):
    placed = (
        P("ment", None, None),
        P(None, None, "ent"),
        P("ent", None),
        P(),
        P(),
        P("ent", None, None),
        P("ment"),
        P("ment"),
        P("ment"),
        P("ment", None),
    )
    return jax.shard_map(
        on_device,
        mesh=mesh,
        in_specs=placed,
        out_specs=(
            P(("ment", "ent"), None, None),
            P("ment", None, "ent"),
            P("ent", "ment"),
            P(None, "ment"),
            P("ent", "ment", None),
        ),
        check_vma=False,
    )
```

```python
import functools

import jax
import jax.numpy as jnp
from jax import lax
from jax.experimental import pallas as pl
from jax.experimental.pallas import tpu as pltpu
from jax.sharding import PartitionSpec as P

HD = 64
MESH = pl.DeviceIdType.MESH


def _greet_peers(row, me, n):
    barrier = pltpu.get_barrier_semaphore()
    for k in range(1, n):
        pl.semaphore_signal(
            barrier, inc=1, device_id=(row, lax.rem(me + k, n)), device_id_type=MESH
        )
    pl.semaphore_wait(barrier, n - 1)


def _peer_sum_kernel(n, x_ref, out_ref, recv, send_sem, recv_sem, own_sem):
    row = lax.axis_index("ment")
    me = lax.axis_index("ent")
    _greet_peers(row, me, n)
    sends = []
    for k in range(1, n):
        copy = pltpu.make_async_remote_copy(
            src_ref=x_ref,
            dst_ref=recv.at[me],
            send_sem=send_sem.at[k - 1],
            recv_sem=recv_sem.at[me],
            device_id=(row, lax.rem(me + k, n)),
            device_id_type=MESH,
        )
        copy.start()
        sends.append(copy)
    own = pltpu.make_async_copy(x_ref, recv.at[me], own_sem)
    own.start()
    for k in range(1, n):
        source = lax.rem(me + n - k, n)
        pltpu.make_async_remote_copy(
            src_ref=x_ref,
            dst_ref=recv.at[source],
            send_sem=send_sem.at[k - 1],
            recv_sem=recv_sem.at[source],
            device_id=(row, source),
            device_id_type=MESH,
        ).wait_recv()
    own.wait()
    for copy in sends:
        copy.wait_send()
    total = recv[0].astype(jnp.float32)
    for s in range(1, n):
        total = total + recv[s].astype(jnp.float32)
    out_ref[...] = total


def peer_sum(x, collective):
    n = lax.axis_size("ent")
    return pl.pallas_call(
        functools.partial(_peer_sum_kernel, n),
        out_shape=jax.ShapeDtypeStruct(x.shape, jnp.float32),
        in_specs=[pl.BlockSpec(memory_space=pltpu.VMEM)],
        out_specs=pl.BlockSpec(memory_space=pltpu.VMEM),
        scratch_shapes=[
            pltpu.VMEM((n,) + x.shape, x.dtype),
            pltpu.SemaphoreType.DMA((n - 1,)),
            pltpu.SemaphoreType.DMA((n,)),
            pltpu.SemaphoreType.DMA(()),
        ],
        compiler_params=pltpu.CompilerParams(collective_id=collective, has_side_effects=True),
    )(x)


def _peer_scatter_kernel(n, y_ref, resid_ref, out_ref, recv, send_sem, recv_sem, own_sem):
    row = lax.axis_index("ment")
    me = lax.axis_index("ent")
    share = out_ref.shape[0]
    _greet_peers(row, me, n)
    sends = []
    for k in range(1, n):
        target = lax.rem(me + k, n)
        copy = pltpu.make_async_remote_copy(
            src_ref=y_ref.at[pl.ds(target * share, share)],
            dst_ref=recv.at[me],
            send_sem=send_sem.at[k - 1],
            recv_sem=recv_sem.at[me],
            device_id=(row, target),
            device_id_type=MESH,
        )
        copy.start()
        sends.append(copy)
    own = pltpu.make_async_copy(y_ref.at[pl.ds(me * share, share)], recv.at[me], own_sem)
    own.start()
    for k in range(1, n):
        source = lax.rem(me + n - k, n)
        pltpu.make_async_remote_copy(
            src_ref=y_ref.at[pl.ds(0, share)],
            dst_ref=recv.at[source],
            send_sem=send_sem.at[k - 1],
            recv_sem=recv_sem.at[source],
            device_id=(row, source),
            device_id_type=MESH,
        ).wait_recv()
    own.wait()
    for copy in sends:
        copy.wait_send()
    first = lax.broadcasted_iota(jnp.int32, out_ref.shape[1:], 0) == 0

    def one_mention(i, carry):
        total = recv[0, i].astype(jnp.float32)
        for s in range(1, n):
            total = total + recv[s, i].astype(jnp.float32)
        total = total + jnp.where(first, resid_ref[pl.ds(i, 1), :], 0.0)
        out_ref[i] = total.astype(out_ref.dtype)
        return carry

    lax.fori_loop(0, share, one_mention, 0)


def peer_scatter(y, resid, collective):
    n = lax.axis_size("ent")
    share = y.shape[0] // n
    return pl.pallas_call(
        functools.partial(_peer_scatter_kernel, n),
        out_shape=jax.ShapeDtypeStruct((share,) + y.shape[1:], jnp.bfloat16),
        in_specs=[pl.BlockSpec(memory_space=pltpu.VMEM)] * 2,
        out_specs=pl.BlockSpec(memory_space=pltpu.VMEM),
        scratch_shapes=[
            pltpu.VMEM((n, share) + y.shape[1:], y.dtype),
            pltpu.SemaphoreType.DMA((n - 1,)),
            pltpu.SemaphoreType.DMA((n,)),
            pltpu.SemaphoreType.DMA(()),
        ],
        compiler_params=pltpu.CompilerParams(collective_id=collective, has_side_effects=True),
    )(y, resid)


ln_eps = 1e-06


def contract(left, right, left_dim, right_dim):
    return lax.dot_general(
        left, right, (((left_dim,), (right_dim,)), ((), ())), preferred_element_type=jnp.float32
    )


def on_device(
    hidden_in, w_qkv, w_out, ln_gain, ln_bias, table, key_len, gold_block, gold_row, neg_blocks
):
    ment_rows, seq_len, width = hidden_in.shape
    local_cols = w_qkv.shape[2]
    local_heads = local_cols // HD
    own_blocks, block_rows = (table.shape[0], table.shape[1])
    score_scale = HD ** (-0.5)
    owner = lax.axis_index("ent")
    first_block = owner * own_blocks
    cls_rows = hidden_in[:, 0, :]
    w_query = w_qkv[:, 0, :]
    w_keyval = w_qkv[:, 1:, :].reshape(width, 2 * local_cols)
    query = jnp.dot(cls_rows, w_query, preferred_element_type=jnp.float32).astype(jnp.bfloat16)
    keyval = jnp.dot(
        hidden_in.reshape(ment_rows * seq_len, width), w_keyval, preferred_element_type=jnp.float32
    )
    keyval = keyval.astype(jnp.bfloat16).reshape(ment_rows, seq_len, 2, local_heads, HD)
    key_heads = keyval[:, :, 0]
    value_heads = keyval[:, :, 1]
    query_heads = query.reshape(ment_rows, local_heads, HD)
    attention_scores = (
        jnp.einsum("ybn,yqbn->ybq", query_heads, key_heads, preferred_element_type=jnp.float32)
        * score_scale
    )
    valid = (jnp.arange(seq_len, dtype=jnp.int32)[None, :] < key_len[:, None]).astype(jnp.float32)
    expo = jnp.exp(attention_scores) * valid[:, None, :]
    probs = expo / jnp.sum(expo, axis=-1, keepdims=True)
    probability_half = probs.astype(jnp.bfloat16)
    context_rows = jnp.einsum(
        "qjp,qpjb->qjb", probability_half, value_heads, preferred_element_type=jnp.float32
    )
    context_rows = context_rows.reshape(ment_rows, local_cols).astype(jnp.bfloat16)
    attn_part = jnp.dot(context_rows, w_out, preferred_element_type=jnp.float32)
    local_block = gold_block - first_block
    owned = (local_block >= 0) & (local_block < own_blocks)
    safe_block = jnp.clip(local_block, 0, own_blocks - 1)
    flat_table = table.reshape(own_blocks * block_rows, width)
    picked = flat_table[safe_block * block_rows + gold_row]
    picked = jnp.where(owned[:, None], picked.astype(jnp.float32), 0.0)
    both = peer_sum(
        jnp.concatenate([attn_part.astype(jnp.bfloat16), picked.astype(jnp.bfloat16)], axis=0), 0
    )
    attn_out, gold_sum = both[:ment_rows], both[ment_rows:]
    golds = gold_sum.astype(jnp.bfloat16)
    resid = cls_rows.astype(jnp.float32) + attn_out
    centre = resid - jnp.mean(resid, axis=-1, keepdims=True)
    rstd = lax.rsqrt(jnp.mean(centre * centre, axis=-1, keepdims=True) + ln_eps)
    normed = centre * rstd
    embed = (normed * ln_gain + ln_bias).astype(jnp.bfloat16)
    inbatch = contract(embed, golds, 1, 1)
    negscore = contract(embed, flat_table, 1, 1)
    block_ids = first_block + jnp.arange(own_blocks, dtype=jnp.int32)
    listed = jnp.any(neg_blocks[0][:, None] == block_ids[None, :], axis=0).astype(jnp.float32)
    row_mask = jnp.repeat(listed, block_rows)
    neg_part = jnp.sum(jnp.exp(negscore) * row_mask[None, :], axis=1)
    neg_total = peer_sum(jnp.pad(neg_part.reshape(1, ment_rows), ((0, 7), (0, 0))), 1)[0]
    lse = jnp.log(jnp.sum(jnp.exp(inbatch), axis=1) + neg_total)
    eye = jnp.eye(ment_rows, dtype=jnp.float32)
    w_inb = (jnp.exp(inbatch - lse[:, None]) - eye).astype(jnp.bfloat16)
    w_neg = (jnp.exp(negscore - lse[:, None]) * row_mask[None, :]).astype(jnp.bfloat16)
    embed_part = jnp.dot(w_neg, flat_table, preferred_element_type=jnp.float32)
    d_embed = jnp.dot(w_inb, golds, preferred_element_type=jnp.float32) + peer_sum(
        embed_part.astype(jnp.bfloat16), 2
    )
    ln_terms = jnp.stack([jnp.sum(d_embed * normed, axis=0), jnp.sum(d_embed, axis=0)])
    upper = d_embed * ln_gain
    d_resid = rstd * (
        upper
        - jnp.mean(upper, axis=-1, keepdims=True)
        - normed * jnp.mean(upper * normed, axis=-1, keepdims=True)
    )
    d_resid_bf = d_resid.astype(jnp.bfloat16)
    wo_term = contract(context_rows, d_resid_bf, 0, 0)
    d_context = contract(d_resid_bf, w_out, 1, 1).astype(jnp.bfloat16)
    context_head_gradient = d_context.reshape(ment_rows, local_heads, HD)
    probability_gradient = jnp.einsum(
        "ybn,yqbn->ybq", context_head_gradient, value_heads, preferred_element_type=jnp.float32
    )
    score_gradient = probs * (
        probability_gradient - jnp.sum(probs * probability_gradient, axis=-1, keepdims=True)
    )
    query_gradient = (
        jnp.einsum("qjp,qpjb->qjb", score_gradient, key_heads, preferred_element_type=jnp.float32)
        * score_scale
    )
    query_gradient = query_gradient.reshape(ment_rows, local_cols).astype(jnp.bfloat16)
    key_gradient = (
        jnp.einsum("ryk,ryo->rkyo", score_gradient, query_heads, preferred_element_type=jnp.float32)
        * score_scale
    )
    value_gradient = jnp.einsum(
        "ryk,ryo->rkyo", probability_half, context_head_gradient, preferred_element_type=jnp.float32
    )
    d_keyval = (
        jnp.stack([key_gradient, value_gradient], axis=2)
        .reshape(ment_rows, seq_len, 2 * local_cols)
        .astype(jnp.bfloat16)
    )
    flat_grad = d_keyval.reshape(ment_rows * seq_len, 2 * local_cols)
    count = lax.axis_size("ment") * (width // lax.axis_size("ment"))
    kv_term = contract(hidden_in.reshape(ment_rows * seq_len, count), flat_grad, 0, 0)
    query_term = contract(hidden_in[:, 0, :], query_gradient, 0, 0)
    qkv_term = jnp.concatenate(
        [query_term[:, None, :], kv_term.reshape(count, 2, local_cols)], axis=1
    )
    share = ment_rows // lax.axis_size("ent")
    grad_part = d_keyval.reshape(share * lax.axis_size("ent") * seq_len, 2 * local_cols)
    token_term = contract(grad_part, w_keyval, 1, 1).reshape(
        share * lax.axis_size("ent"), seq_len, width
    )
    resid_mine = lax.dynamic_slice_in_dim(d_resid, owner * share, share, 0)
    grad_hidden = peer_scatter(
        token_term.at[:, 0, :].add(contract(query_gradient, w_query, 1, 1)).astype(jnp.bfloat16),
        resid_mine,
        3,
    )
    gold_terms = contract(w_inb, embed, 0, 0)
    weight_blocks = w_neg.reshape(ment_rows, own_blocks, block_rows)
    count = lax.axis_size("ment") * (block_rows // lax.axis_size("ment"))
    neg_term = jnp.einsum("mbr,md->rbd", weight_blocks, embed, preferred_element_type=jnp.float32)
    inside = owned & (gold_row >= 0) & (gold_row < count)
    row_slot = jnp.where(inside, gold_row, count)
    table_term = neg_term.at[row_slot, safe_block].add(gold_terms, mode="drop")
    parts = lax.axis_size("ment")
    qkv_rows = width // parts
    wo_cols = width // parts
    tab_rows = block_rows // parts
    pieces = [
        qkv_term.reshape(parts, qkv_rows * 3 * local_cols),
        wo_term.reshape(local_cols, parts, wo_cols).transpose(1, 0, 2).reshape(parts, -1),
        table_term.reshape(parts, tab_rows, own_blocks, width)
        .transpose(0, 2, 1, 3)
        .reshape(parts, -1),
        ln_terms.reshape(2, parts, wo_cols).transpose(1, 0, 2).reshape(parts, -1),
    ]
    sizes = [piece.shape[1] for piece in pieces]
    padded = -sum(sizes) % 1024
    pieces.append(jnp.zeros((parts, padded), jnp.float32))
    stacked = jnp.concatenate(pieces, axis=1).reshape(parts * 8, -1)
    merged = lax.psum_scatter(stacked, "ment", scatter_dimension=0, tiled=True).reshape(-1)
    offsets = [sum(sizes[:k]) for k in range(len(sizes))]
    grad_qkv = merged[offsets[0] : offsets[0] + sizes[0]].reshape(qkv_rows, 3, local_cols)
    grad_wo = merged[offsets[1] : offsets[1] + sizes[1]].reshape(local_cols, wo_cols)
    grad_table = merged[offsets[2] : offsets[2] + sizes[2]].reshape(own_blocks, tab_rows, width)
    grad_ln = merged[offsets[3] : offsets[3] + sizes[3]].reshape(2, wo_cols)
    return (grad_hidden, grad_qkv, grad_wo, grad_ln, grad_table)


def solution(mesh):
    placed = (
        P("ment", None, None),
        P(None, None, "ent"),
        P("ent", None),
        P(),
        P(),
        P("ent", None, None),
        P("ment"),
        P("ment"),
        P("ment"),
        P("ment", None),
    )
    return jax.shard_map(
        on_device,
        mesh=mesh,
        in_specs=placed,
        out_specs=(
            P(("ment", "ent"), None, None),
            P("ment", None, "ent"),
            P("ent", "ment"),
            P(None, "ment"),
            P("ent", "ment", None),
        ),
        check_vma=False,
    )
```

```python
import functools

import jax
import jax.numpy as jnp
from jax import lax
from jax.experimental import pallas as pl
from jax.experimental.pallas import tpu as pltpu
from jax.sharding import PartitionSpec as P

HD = 64
MESH = pl.DeviceIdType.MESH


def _greet_peers(row, me, n):
    barrier = pltpu.get_barrier_semaphore()
    for k in range(1, n):
        pl.semaphore_signal(
            barrier, inc=1, device_id=(row, lax.rem(me + k, n)), device_id_type=MESH
        )
    pl.semaphore_wait(barrier, n - 1)


def _peer_sum_kernel(n, x_ref, out_ref, recv, send_sem, recv_sem, own_sem):
    row = lax.axis_index("ment")
    me = lax.axis_index("ent")
    _greet_peers(row, me, n)
    sends = []
    for k in range(1, n):
        copy = pltpu.make_async_remote_copy(
            src_ref=x_ref,
            dst_ref=recv.at[me],
            send_sem=send_sem.at[k - 1],
            recv_sem=recv_sem.at[me],
            device_id=(row, lax.rem(me + k, n)),
            device_id_type=MESH,
        )
        copy.start()
        sends.append(copy)
    own = pltpu.make_async_copy(x_ref, recv.at[me], own_sem)
    own.start()
    for k in range(1, n):
        source = lax.rem(me + n - k, n)
        pltpu.make_async_remote_copy(
            src_ref=x_ref,
            dst_ref=recv.at[source],
            send_sem=send_sem.at[k - 1],
            recv_sem=recv_sem.at[source],
            device_id=(row, source),
            device_id_type=MESH,
        ).wait_recv()
    own.wait()
    for copy in sends:
        copy.wait_send()
    total = recv[0].astype(jnp.float32)
    for s in range(1, n):
        total = total + recv[s].astype(jnp.float32)
    out_ref[...] = total


def peer_sum(x, collective):
    n = lax.axis_size("ent")
    return pl.pallas_call(
        functools.partial(_peer_sum_kernel, n),
        out_shape=jax.ShapeDtypeStruct(x.shape, jnp.float32),
        in_specs=[pl.BlockSpec(memory_space=pltpu.VMEM)],
        out_specs=pl.BlockSpec(memory_space=pltpu.VMEM),
        scratch_shapes=[
            pltpu.VMEM((n,) + x.shape, x.dtype),
            pltpu.SemaphoreType.DMA((n - 1,)),
            pltpu.SemaphoreType.DMA((n,)),
            pltpu.SemaphoreType.DMA(()),
        ],
        compiler_params=pltpu.CompilerParams(collective_id=collective, has_side_effects=True),
    )(x)


def _peer_scatter_kernel(n, y_ref, resid_ref, out_ref, recv, send_sem, recv_sem, own_sem):
    row = lax.axis_index("ment")
    me = lax.axis_index("ent")
    share = out_ref.shape[0]
    _greet_peers(row, me, n)
    sends = []
    for k in range(1, n):
        target = lax.rem(me + k, n)
        copy = pltpu.make_async_remote_copy(
            src_ref=y_ref.at[pl.ds(target * share, share)],
            dst_ref=recv.at[me],
            send_sem=send_sem.at[k - 1],
            recv_sem=recv_sem.at[me],
            device_id=(row, target),
            device_id_type=MESH,
        )
        copy.start()
        sends.append(copy)
    own = pltpu.make_async_copy(y_ref.at[pl.ds(me * share, share)], recv.at[me], own_sem)
    own.start()
    for k in range(1, n):
        source = lax.rem(me + n - k, n)
        pltpu.make_async_remote_copy(
            src_ref=y_ref.at[pl.ds(0, share)],
            dst_ref=recv.at[source],
            send_sem=send_sem.at[k - 1],
            recv_sem=recv_sem.at[source],
            device_id=(row, source),
            device_id_type=MESH,
        ).wait_recv()
    own.wait()
    for copy in sends:
        copy.wait_send()
    first = lax.broadcasted_iota(jnp.int32, out_ref.shape[1:], 0) == 0

    def one_mention(i, carry):
        total = recv[0, i].astype(jnp.float32)
        for s in range(1, n):
            total = total + recv[s, i].astype(jnp.float32)
        total = total + jnp.where(first, resid_ref[pl.ds(i, 1), :], 0.0)
        out_ref[i] = total.astype(out_ref.dtype)
        return carry

    lax.fori_loop(0, share, one_mention, 0)


def peer_scatter(y, resid, collective):
    n = lax.axis_size("ent")
    share = y.shape[0] // n
    return pl.pallas_call(
        functools.partial(_peer_scatter_kernel, n),
        out_shape=jax.ShapeDtypeStruct((share,) + y.shape[1:], jnp.bfloat16),
        in_specs=[pl.BlockSpec(memory_space=pltpu.VMEM)] * 2,
        out_specs=pl.BlockSpec(memory_space=pltpu.VMEM),
        scratch_shapes=[
            pltpu.VMEM((n, share) + y.shape[1:], y.dtype),
            pltpu.SemaphoreType.DMA((n - 1,)),
            pltpu.SemaphoreType.DMA((n,)),
            pltpu.SemaphoreType.DMA(()),
        ],
        compiler_params=pltpu.CompilerParams(collective_id=collective, has_side_effects=True),
    )(y, resid)


ln_eps = 1e-06


def contract(left, right, left_dim, right_dim):
    return lax.dot_general(
        left, right, (((left_dim,), (right_dim,)), ((), ())), preferred_element_type=jnp.float32
    )


def on_device(
    hidden_in, w_qkv, w_out, ln_gain, ln_bias, table, key_len, gold_block, gold_row, neg_blocks
):
    ment_rows, seq_len, width = hidden_in.shape
    local_cols = w_qkv.shape[2]
    local_heads = local_cols // HD
    own_blocks, block_rows = (table.shape[0], table.shape[1])
    score_scale = HD ** (-0.5)
    owner = lax.axis_index("ent")
    first_block = owner * own_blocks
    cls_rows = hidden_in[:, 0, :]
    w_query = w_qkv[:, 0, :]
    w_keyval = w_qkv[:, 1:, :].reshape(width, 2 * local_cols)
    query = jnp.dot(cls_rows, w_query, preferred_element_type=jnp.float32).astype(jnp.bfloat16)
    keyval = jnp.dot(
        hidden_in.reshape(ment_rows * seq_len, width), w_keyval, preferred_element_type=jnp.float32
    )
    keyval = keyval.astype(jnp.bfloat16).reshape(ment_rows, seq_len, 2, local_heads, HD)
    key_heads = keyval[:, :, 0]
    value_heads = keyval[:, :, 1]
    query_heads = query.reshape(ment_rows, local_heads, HD)
    attention_scores = (
        jnp.einsum("ybn,yqbn->ybq", query_heads, key_heads, preferred_element_type=jnp.float32)
        * score_scale
    )
    valid = (jnp.arange(seq_len, dtype=jnp.int32)[None, :] < key_len[:, None]).astype(jnp.float32)
    expo = jnp.exp(attention_scores) * valid[:, None, :]
    probs = expo / jnp.sum(expo, axis=-1, keepdims=True)
    probability_half = probs.astype(jnp.bfloat16)
    context_rows = jnp.einsum(
        "qjp,qpjb->qjb", probability_half, value_heads, preferred_element_type=jnp.float32
    )
    context_rows = context_rows.reshape(ment_rows, local_cols).astype(jnp.bfloat16)
    attn_part = jnp.dot(context_rows, w_out, preferred_element_type=jnp.float32)
    local_block = gold_block - first_block
    owned = (local_block >= 0) & (local_block < own_blocks)
    safe_block = jnp.clip(local_block, 0, own_blocks - 1)
    flat_table = table.reshape(own_blocks * block_rows, width)
    picked = flat_table[safe_block * block_rows + gold_row]
    picked = jnp.where(owned[:, None], picked.astype(jnp.float32), 0.0)
    both = peer_sum(
        jnp.concatenate([attn_part.astype(jnp.bfloat16), picked.astype(jnp.bfloat16)], axis=0), 0
    )
    attn_out, gold_sum = both[:ment_rows], both[ment_rows:]
    golds = gold_sum.astype(jnp.bfloat16)
    resid = cls_rows.astype(jnp.float32) + attn_out
    centre = resid - jnp.mean(resid, axis=-1, keepdims=True)
    rstd = lax.rsqrt(jnp.mean(centre * centre, axis=-1, keepdims=True) + ln_eps)
    normed = centre * rstd
    embed = (normed * ln_gain + ln_bias).astype(jnp.bfloat16)
    inbatch = contract(embed, golds, 1, 1)
    negscore = contract(embed, flat_table, 1, 1)
    block_ids = first_block + jnp.arange(own_blocks, dtype=jnp.int32)
    listed = jnp.any(neg_blocks[0][:, None] == block_ids[None, :], axis=0).astype(jnp.float32)
    row_mask = jnp.repeat(listed, block_rows)
    neg_part = jnp.sum(jnp.exp(negscore) * row_mask[None, :], axis=1)
    neg_total = peer_sum(jnp.pad(neg_part.reshape(1, ment_rows), ((0, 7), (0, 0))), 1)[0]
    lse = jnp.log(jnp.sum(jnp.exp(inbatch), axis=1) + neg_total)
    eye = jnp.eye(ment_rows, dtype=jnp.float32)
    w_inb = (jnp.exp(inbatch - lse[:, None]) - eye).astype(jnp.bfloat16)
    w_neg = (jnp.exp(negscore - lse[:, None]) * row_mask[None, :]).astype(jnp.bfloat16)
    embed_part = jnp.dot(w_neg, flat_table, preferred_element_type=jnp.float32)
    d_embed = jnp.dot(w_inb, golds, preferred_element_type=jnp.float32) + peer_sum(
        embed_part.astype(jnp.bfloat16), 2
    )
    ln_terms = jnp.stack([jnp.sum(d_embed * normed, axis=0), jnp.sum(d_embed, axis=0)])
    upper = d_embed * ln_gain
    d_resid = rstd * (
        upper
        - jnp.mean(upper, axis=-1, keepdims=True)
        - normed * jnp.mean(upper * normed, axis=-1, keepdims=True)
    )
    d_resid_bf = d_resid.astype(jnp.bfloat16)
    wo_term = contract(context_rows, d_resid_bf, 0, 0)
    d_context = contract(d_resid_bf, w_out, 1, 1).astype(jnp.bfloat16)
    context_head_gradient = d_context.reshape(ment_rows, local_heads, HD)
    probability_gradient = jnp.einsum(
        "ybn,yqbn->ybq", context_head_gradient, value_heads, preferred_element_type=jnp.float32
    )
    score_gradient = probs * (
        probability_gradient - jnp.sum(probs * probability_gradient, axis=-1, keepdims=True)
    )
    query_gradient = (
        jnp.einsum("qjp,qpjb->qjb", score_gradient, key_heads, preferred_element_type=jnp.float32)
        * score_scale
    )
    query_gradient = query_gradient.reshape(ment_rows, local_cols).astype(jnp.bfloat16)
    key_gradient = (
        jnp.einsum("ryk,ryo->rkyo", score_gradient, query_heads, preferred_element_type=jnp.float32)
        * score_scale
    )
    value_gradient = jnp.einsum(
        "ryk,ryo->rkyo", probability_half, context_head_gradient, preferred_element_type=jnp.float32
    )
    d_keyval = (
        jnp.stack([key_gradient, value_gradient], axis=2)
        .reshape(ment_rows, seq_len, 2 * local_cols)
        .astype(jnp.bfloat16)
    )
    flat_grad = d_keyval.reshape(ment_rows * seq_len, 2 * local_cols)
    count = lax.axis_size("ment") * (width // lax.axis_size("ment"))
    kv_term = contract(hidden_in.reshape(ment_rows * seq_len, count), flat_grad, 0, 0)
    query_term = contract(hidden_in[:, 0, :], query_gradient, 0, 0)
    qkv_term = jnp.concatenate(
        [query_term[:, None, :], kv_term.reshape(count, 2, local_cols)], axis=1
    )
    share = ment_rows // lax.axis_size("ent")
    grad_part = d_keyval.reshape(share * lax.axis_size("ent") * seq_len, 2 * local_cols)
    token_term = contract(grad_part, w_keyval, 1, 1).reshape(
        share * lax.axis_size("ent"), seq_len, width
    )
    resid_mine = lax.dynamic_slice_in_dim(d_resid, owner * share, share, 0)
    grad_hidden = peer_scatter(
        token_term.at[:, 0, :].add(contract(query_gradient, w_query, 1, 1)).astype(jnp.bfloat16),
        resid_mine,
        3,
    )
    gold_terms = contract(w_inb, embed, 0, 0)
    weight_blocks = w_neg.reshape(ment_rows, own_blocks, block_rows)
    count = lax.axis_size("ment") * (block_rows // lax.axis_size("ment"))
    neg_term = jnp.einsum("mbr,md->rbd", weight_blocks, embed, preferred_element_type=jnp.float32)
    inside = owned & (gold_row >= 0) & (gold_row < count)
    row_slot = jnp.where(inside, gold_row, count)
    table_term = neg_term.at[row_slot, safe_block].add(gold_terms, mode="drop")
    parts = lax.axis_size("ment")
    place = lax.axis_index("ment")
    qkv_rows = width // parts
    wo_cols = width // parts
    tab_rows = block_rows // parts
    terms = (qkv_term, wo_term, table_term, ln_terms)
    summed_all = lax.psum(jnp.concatenate([term.reshape(-1) for term in terms]), "ment")
    sums, at = [], 0
    for term in terms:
        sums.append(summed_all[at : at + term.size].reshape(term.shape))
        at += term.size
    qkv_sum, wo_sum, table_sum, ln_sum = sums
    grad_qkv = lax.dynamic_slice_in_dim(qkv_sum, place * qkv_rows, qkv_rows, 0)
    grad_wo = lax.dynamic_slice_in_dim(wo_sum, place * wo_cols, wo_cols, 1)
    grad_ln = lax.dynamic_slice_in_dim(ln_sum, place * wo_cols, wo_cols, 1)
    grad_table = jnp.transpose(
        lax.dynamic_slice_in_dim(table_sum, place * tab_rows, tab_rows, 0), (1, 0, 2)
    )
    return (grad_hidden, grad_qkv, grad_wo, grad_ln, grad_table)


def solution(mesh):
    placed = (
        P("ment", None, None),
        P(None, None, "ent"),
        P("ent", None),
        P(),
        P(),
        P("ent", None, None),
        P("ment"),
        P("ment"),
        P("ment"),
        P("ment", None),
    )
    return jax.shard_map(
        on_device,
        mesh=mesh,
        in_specs=placed,
        out_specs=(
            P(("ment", "ent"), None, None),
            P("ment", None, "ent"),
            P("ent", "ment"),
            P(None, "ment"),
            P("ent", "ment", None),
        ),
        check_vma=False,
    )
```

```python
import functools

import jax
import jax.numpy as jnp
from jax import lax
from jax.experimental import pallas as pl
from jax.experimental.pallas import tpu as pltpu
from jax.sharding import PartitionSpec as P

HD = 64
MESH = pl.DeviceIdType.MESH


def _greet_peers(row, me, n):
    barrier = pltpu.get_barrier_semaphore()
    for k in range(1, n):
        pl.semaphore_signal(
            barrier, inc=1, device_id=(row, lax.rem(me + k, n)), device_id_type=MESH
        )
    pl.semaphore_wait(barrier, n - 1)


def _peer_sum_kernel(n, x_ref, out_ref, recv, send_sem, recv_sem, own_sem):
    row = lax.axis_index("ment")
    me = lax.axis_index("ent")
    _greet_peers(row, me, n)
    sends = []
    for k in range(1, n):
        copy = pltpu.make_async_remote_copy(
            src_ref=x_ref,
            dst_ref=recv.at[me],
            send_sem=send_sem.at[k - 1],
            recv_sem=recv_sem.at[me],
            device_id=(row, lax.rem(me + k, n)),
            device_id_type=MESH,
        )
        copy.start()
        sends.append(copy)
    own = pltpu.make_async_copy(x_ref, recv.at[me], own_sem)
    own.start()
    for k in range(1, n):
        source = lax.rem(me + n - k, n)
        pltpu.make_async_remote_copy(
            src_ref=x_ref,
            dst_ref=recv.at[source],
            send_sem=send_sem.at[k - 1],
            recv_sem=recv_sem.at[source],
            device_id=(row, source),
            device_id_type=MESH,
        ).wait_recv()
    own.wait()
    for copy in sends:
        copy.wait_send()
    total = recv[0].astype(jnp.float32)
    for s in range(1, n):
        total = total + recv[s].astype(jnp.float32)
    out_ref[...] = total


def peer_sum(x, collective):
    n = lax.axis_size("ent")
    return pl.pallas_call(
        functools.partial(_peer_sum_kernel, n),
        out_shape=jax.ShapeDtypeStruct(x.shape, jnp.float32),
        in_specs=[pl.BlockSpec(memory_space=pltpu.VMEM)],
        out_specs=pl.BlockSpec(memory_space=pltpu.VMEM),
        scratch_shapes=[
            pltpu.VMEM((n,) + x.shape, x.dtype),
            pltpu.SemaphoreType.DMA((n - 1,)),
            pltpu.SemaphoreType.DMA((n,)),
            pltpu.SemaphoreType.DMA(()),
        ],
        compiler_params=pltpu.CompilerParams(collective_id=collective, has_side_effects=True),
    )(x)


def _peer_scatter_kernel(n, y_ref, resid_ref, out_ref, recv, send_sem, recv_sem, own_sem):
    row = lax.axis_index("ment")
    me = lax.axis_index("ent")
    share = out_ref.shape[0]
    _greet_peers(row, me, n)
    sends = []
    for k in range(1, n):
        target = lax.rem(me + k, n)
        copy = pltpu.make_async_remote_copy(
            src_ref=y_ref.at[pl.ds(target * share, share)],
            dst_ref=recv.at[me],
            send_sem=send_sem.at[k - 1],
            recv_sem=recv_sem.at[me],
            device_id=(row, target),
            device_id_type=MESH,
        )
        copy.start()
        sends.append(copy)
    own = pltpu.make_async_copy(y_ref.at[pl.ds(me * share, share)], recv.at[me], own_sem)
    own.start()
    for k in range(1, n):
        source = lax.rem(me + n - k, n)
        pltpu.make_async_remote_copy(
            src_ref=y_ref.at[pl.ds(0, share)],
            dst_ref=recv.at[source],
            send_sem=send_sem.at[k - 1],
            recv_sem=recv_sem.at[source],
            device_id=(row, source),
            device_id_type=MESH,
        ).wait_recv()
    own.wait()
    for copy in sends:
        copy.wait_send()
    first = lax.broadcasted_iota(jnp.int32, out_ref.shape[1:], 0) == 0

    def one_mention(i, carry):
        total = recv[0, i].astype(jnp.float32)
        for s in range(1, n):
            total = total + recv[s, i].astype(jnp.float32)
        total = total + jnp.where(first, resid_ref[pl.ds(i, 1), :], 0.0)
        out_ref[i] = total.astype(out_ref.dtype)
        return carry

    lax.fori_loop(0, share, one_mention, 0)


def peer_scatter(y, resid, collective):
    n = lax.axis_size("ent")
    share = y.shape[0] // n
    return pl.pallas_call(
        functools.partial(_peer_scatter_kernel, n),
        out_shape=jax.ShapeDtypeStruct((share,) + y.shape[1:], jnp.bfloat16),
        in_specs=[pl.BlockSpec(memory_space=pltpu.VMEM)] * 2,
        out_specs=pl.BlockSpec(memory_space=pltpu.VMEM),
        scratch_shapes=[
            pltpu.VMEM((n, share) + y.shape[1:], y.dtype),
            pltpu.SemaphoreType.DMA((n - 1,)),
            pltpu.SemaphoreType.DMA((n,)),
            pltpu.SemaphoreType.DMA(()),
        ],
        compiler_params=pltpu.CompilerParams(collective_id=collective, has_side_effects=True),
    )(y, resid)


ln_eps = 1e-06


def contract(left, right, left_dim, right_dim):
    return lax.dot_general(
        left, right, (((left_dim,), (right_dim,)), ((), ())), preferred_element_type=jnp.float32
    )


def on_device(
    hidden_in, w_qkv, w_out, ln_gain, ln_bias, table, key_len, gold_block, gold_row, neg_blocks
):
    ment_rows, seq_len, width = hidden_in.shape
    local_cols = w_qkv.shape[2]
    local_heads = local_cols // HD
    own_blocks, block_rows = (table.shape[0], table.shape[1])
    score_scale = HD ** (-0.5)
    owner = lax.axis_index("ent")
    first_block = owner * own_blocks
    cls_rows = hidden_in[:, 0, :]
    w_query = w_qkv[:, 0, :]
    w_keyval = w_qkv[:, 1:, :].reshape(width, 2 * local_cols)
    query = jnp.dot(cls_rows, w_query, preferred_element_type=jnp.float32).astype(jnp.bfloat16)
    keyval = jnp.dot(
        hidden_in.reshape(ment_rows * seq_len, width), w_keyval, preferred_element_type=jnp.float32
    )
    keyval = keyval.astype(jnp.bfloat16).reshape(ment_rows, seq_len, 2, local_heads, HD)
    key_heads = keyval[:, :, 0]
    value_heads = keyval[:, :, 1]
    query_heads = query.reshape(ment_rows, local_heads, HD)
    attention_scores = (
        jnp.einsum("ybn,yqbn->ybq", query_heads, key_heads, preferred_element_type=jnp.float32)
        * score_scale
    )
    valid = (jnp.arange(seq_len, dtype=jnp.int32)[None, :] < key_len[:, None]).astype(jnp.float32)
    expo = jnp.exp(attention_scores) * valid[:, None, :]
    probs = expo / jnp.sum(expo, axis=-1, keepdims=True)
    probability_half = probs.astype(jnp.bfloat16)
    context_rows = jnp.einsum(
        "qjp,qpjb->qjb", probability_half, value_heads, preferred_element_type=jnp.float32
    )
    context_rows = context_rows.reshape(ment_rows, local_cols).astype(jnp.bfloat16)
    attn_part = jnp.dot(context_rows, w_out, preferred_element_type=jnp.float32)
    local_block = gold_block - first_block
    owned = (local_block >= 0) & (local_block < own_blocks)
    safe_block = jnp.clip(local_block, 0, own_blocks - 1)
    flat_table = table.reshape(own_blocks * block_rows, width)
    picked = flat_table[safe_block * block_rows + gold_row]
    picked = jnp.where(owned[:, None], picked.astype(jnp.float32), 0.0)
    both = peer_sum(
        jnp.concatenate([attn_part.astype(jnp.bfloat16), picked.astype(jnp.bfloat16)], axis=0), 0
    )
    attn_out, gold_sum = both[:ment_rows], both[ment_rows:]
    golds = gold_sum.astype(jnp.bfloat16)
    resid = cls_rows.astype(jnp.float32) + attn_out
    centre = resid - jnp.mean(resid, axis=-1, keepdims=True)
    rstd = lax.rsqrt(jnp.mean(centre * centre, axis=-1, keepdims=True) + ln_eps)
    normed = centre * rstd
    embed = (normed * ln_gain + ln_bias).astype(jnp.bfloat16)
    inbatch = contract(embed, golds, 1, 1)
    negscore = contract(embed, flat_table, 1, 1)
    block_ids = first_block + jnp.arange(own_blocks, dtype=jnp.int32)
    listed = jnp.any(neg_blocks[0][:, None] == block_ids[None, :], axis=0).astype(jnp.float32)
    row_mask = jnp.repeat(listed, block_rows)
    neg_part = jnp.sum(jnp.exp(negscore) * row_mask[None, :], axis=1)
    neg_total = peer_sum(jnp.pad(neg_part.reshape(1, ment_rows), ((0, 7), (0, 0))), 1)[0]
    lse = jnp.log(jnp.sum(jnp.exp(inbatch), axis=1) + neg_total)
    eye = jnp.eye(ment_rows, dtype=jnp.float32)
    w_inb = (jnp.exp(inbatch - lse[:, None]) - eye).astype(jnp.bfloat16)
    w_neg = (jnp.exp(negscore - lse[:, None]) * row_mask[None, :]).astype(jnp.bfloat16)
    embed_part = jnp.dot(w_neg, flat_table, preferred_element_type=jnp.float32)
    d_embed = jnp.dot(w_inb, golds, preferred_element_type=jnp.float32) + peer_sum(
        embed_part.astype(jnp.bfloat16), 2
    )
    ln_terms = jnp.stack([jnp.sum(d_embed * normed, axis=0), jnp.sum(d_embed, axis=0)])
    upper = d_embed * ln_gain
    d_resid = rstd * (
        upper
        - jnp.mean(upper, axis=-1, keepdims=True)
        - normed * jnp.mean(upper * normed, axis=-1, keepdims=True)
    )
    d_resid_bf = d_resid.astype(jnp.bfloat16)
    wo_term = contract(context_rows, d_resid_bf, 0, 0)
    d_context = contract(d_resid_bf, w_out, 1, 1).astype(jnp.bfloat16)
    context_head_gradient = d_context.reshape(ment_rows, local_heads, HD)
    probability_gradient = jnp.einsum(
        "ybn,yqbn->ybq", context_head_gradient, value_heads, preferred_element_type=jnp.float32
    )
    score_gradient = probs * (
        probability_gradient - jnp.sum(probs * probability_gradient, axis=-1, keepdims=True)
    )
    query_gradient = (
        jnp.einsum("qjp,qpjb->qjb", score_gradient, key_heads, preferred_element_type=jnp.float32)
        * score_scale
    )
    query_gradient = query_gradient.reshape(ment_rows, local_cols).astype(jnp.bfloat16)
    key_gradient = (
        jnp.einsum("ryk,ryo->rkyo", score_gradient, query_heads, preferred_element_type=jnp.float32)
        * score_scale
    )
    value_gradient = jnp.einsum(
        "ryk,ryo->rkyo", probability_half, context_head_gradient, preferred_element_type=jnp.float32
    )
    d_keyval = (
        jnp.stack([key_gradient, value_gradient], axis=2)
        .reshape(ment_rows, seq_len, 2 * local_cols)
        .astype(jnp.bfloat16)
    )
    flat_grad = d_keyval.reshape(ment_rows * seq_len, 2 * local_cols)
    count = lax.axis_size("ment") * (width // lax.axis_size("ment"))
    kv_term = contract(hidden_in.reshape(ment_rows * seq_len, count), flat_grad, 0, 0)
    query_term = contract(hidden_in[:, 0, :], query_gradient, 0, 0)
    qkv_term = jnp.concatenate(
        [query_term[:, None, :], kv_term.reshape(count, 2, local_cols)], axis=1
    )
    share = ment_rows // lax.axis_size("ent")
    grad_part = d_keyval.reshape(share * lax.axis_size("ent") * seq_len, 2 * local_cols)
    token_term = contract(grad_part, w_keyval, 1, 1).reshape(
        share * lax.axis_size("ent"), seq_len, width
    )
    resid_mine = lax.dynamic_slice_in_dim(d_resid, owner * share, share, 0)
    grad_hidden = peer_scatter(
        token_term.at[:, 0, :].add(contract(query_gradient, w_query, 1, 1)).astype(jnp.bfloat16),
        resid_mine,
        3,
    )
    gold_terms = contract(w_inb, embed, 0, 0)
    weight_blocks = w_neg.reshape(ment_rows, own_blocks, block_rows)
    count = lax.axis_size("ment") * (block_rows // lax.axis_size("ment"))
    neg_term = jnp.einsum("mbr,md->rbd", weight_blocks, embed, preferred_element_type=jnp.float32)
    inside = owned & (gold_row >= 0) & (gold_row < count)
    row_slot = jnp.where(inside, gold_row, count)
    table_term = neg_term.at[row_slot, safe_block].add(gold_terms, mode="drop")
    parts = lax.axis_size("ment")
    qkv_rows = width // parts
    wo_cols = width // parts
    tab_rows = block_rows // parts
    pieces = [
        table_term.reshape(parts, -1),
        qkv_term.reshape(parts, -1),
        wo_term.T.reshape(parts, -1),
        ln_terms.T.reshape(parts, -1),
    ]
    sizes = [piece.shape[1] for piece in pieces]
    slab = own_blocks * width
    pieces.append(jnp.zeros((parts, -sum(sizes) % slab), jnp.float32))
    merged = lax.psum_scatter(
        jnp.concatenate(pieces, axis=1).reshape(-1, own_blocks, width),
        "ment",
        scatter_dimension=0,
        tiled=True,
    )
    merged = lax.optimization_barrier(merged).reshape(-1)
    sums, at = [], 0
    for size in sizes:
        sums.append(merged[at : at + size])
        at += size
    grad_table = sums[0].reshape(tab_rows, own_blocks, width).transpose(1, 0, 2)
    grad_qkv = sums[1].reshape(qkv_rows, 3, local_cols)
    grad_wo = sums[2].reshape(wo_cols, local_cols).T
    grad_ln = sums[3].reshape(wo_cols, 2).T
    return (grad_hidden, grad_qkv, grad_wo, grad_ln, grad_table)


def solution(mesh):
    placed = (
        P("ment", None, None),
        P(None, None, "ent"),
        P("ent", None),
        P(),
        P(),
        P("ent", None, None),
        P("ment"),
        P("ment"),
        P("ment"),
        P("ment", None),
    )
    return jax.shard_map(
        on_device,
        mesh=mesh,
        in_specs=placed,
        out_specs=(
            P(("ment", "ent"), None, None),
            P("ment", None, "ent"),
            P("ent", "ment"),
            P(None, "ment"),
            P("ent", "ment", None),
        ),
        check_vma=False,
    )
```

```python
import functools

import jax
import jax.numpy as jnp
from jax import lax
from jax.experimental import pallas as pl
from jax.experimental.pallas import tpu as pltpu
from jax.sharding import PartitionSpec as P

HD = 64
MESH = pl.DeviceIdType.MESH


def _greet_peers(row, me, n):
    barrier = pltpu.get_barrier_semaphore()
    for k in range(1, n):
        pl.semaphore_signal(
            barrier, inc=1, device_id=(row, lax.rem(me + k, n)), device_id_type=MESH
        )
    pl.semaphore_wait(barrier, n - 1)


def _peer_sum_kernel(n, x_ref, out_ref, recv, send_sem, recv_sem, own_sem):
    row = lax.axis_index("ment")
    me = lax.axis_index("ent")
    _greet_peers(row, me, n)
    sends = []
    for k in range(1, n):
        copy = pltpu.make_async_remote_copy(
            src_ref=x_ref,
            dst_ref=recv.at[me],
            send_sem=send_sem.at[k - 1],
            recv_sem=recv_sem.at[me],
            device_id=(row, lax.rem(me + k, n)),
            device_id_type=MESH,
        )
        copy.start()
        sends.append(copy)
    own = pltpu.make_async_copy(x_ref, recv.at[me], own_sem)
    own.start()
    for k in range(1, n):
        source = lax.rem(me + n - k, n)
        pltpu.make_async_remote_copy(
            src_ref=x_ref,
            dst_ref=recv.at[source],
            send_sem=send_sem.at[k - 1],
            recv_sem=recv_sem.at[source],
            device_id=(row, source),
            device_id_type=MESH,
        ).wait_recv()
    own.wait()
    for copy in sends:
        copy.wait_send()
    total = recv[0].astype(jnp.float32)
    for s in range(1, n):
        total = total + recv[s].astype(jnp.float32)
    out_ref[...] = total


def peer_sum(x, collective):
    n = lax.axis_size("ent")
    return pl.pallas_call(
        functools.partial(_peer_sum_kernel, n),
        out_shape=jax.ShapeDtypeStruct(x.shape, jnp.float32),
        in_specs=[pl.BlockSpec(memory_space=pltpu.VMEM)],
        out_specs=pl.BlockSpec(memory_space=pltpu.VMEM),
        scratch_shapes=[
            pltpu.VMEM((n,) + x.shape, x.dtype),
            pltpu.SemaphoreType.DMA((n - 1,)),
            pltpu.SemaphoreType.DMA((n,)),
            pltpu.SemaphoreType.DMA(()),
        ],
        compiler_params=pltpu.CompilerParams(collective_id=collective, has_side_effects=True),
    )(x)


def _peer_scatter_kernel(n, y_ref, resid_ref, out_ref, recv, send_sem, recv_sem, own_sem):
    row = lax.axis_index("ment")
    me = lax.axis_index("ent")
    share = out_ref.shape[0]
    _greet_peers(row, me, n)
    sends = []
    for k in range(1, n):
        target = lax.rem(me + k, n)
        copy = pltpu.make_async_remote_copy(
            src_ref=y_ref.at[pl.ds(target * share, share)],
            dst_ref=recv.at[me],
            send_sem=send_sem.at[k - 1],
            recv_sem=recv_sem.at[me],
            device_id=(row, target),
            device_id_type=MESH,
        )
        copy.start()
        sends.append(copy)
    own = pltpu.make_async_copy(y_ref.at[pl.ds(me * share, share)], recv.at[me], own_sem)
    own.start()
    for k in range(1, n):
        source = lax.rem(me + n - k, n)
        pltpu.make_async_remote_copy(
            src_ref=y_ref.at[pl.ds(0, share)],
            dst_ref=recv.at[source],
            send_sem=send_sem.at[k - 1],
            recv_sem=recv_sem.at[source],
            device_id=(row, source),
            device_id_type=MESH,
        ).wait_recv()
    own.wait()
    for copy in sends:
        copy.wait_send()
    first = lax.broadcasted_iota(jnp.int32, out_ref.shape[1:], 0) == 0

    def one_mention(i, carry):
        total = recv[0, i].astype(jnp.float32)
        for s in range(1, n):
            total = total + recv[s, i].astype(jnp.float32)
        total = total + jnp.where(first, resid_ref[pl.ds(i, 1), :], 0.0)
        out_ref[i] = total.astype(out_ref.dtype)
        return carry

    lax.fori_loop(0, share, one_mention, 0)


def peer_scatter(y, resid, collective):
    n = lax.axis_size("ent")
    share = y.shape[0] // n
    return pl.pallas_call(
        functools.partial(_peer_scatter_kernel, n),
        out_shape=jax.ShapeDtypeStruct((share,) + y.shape[1:], jnp.bfloat16),
        in_specs=[pl.BlockSpec(memory_space=pltpu.VMEM)] * 2,
        out_specs=pl.BlockSpec(memory_space=pltpu.VMEM),
        scratch_shapes=[
            pltpu.VMEM((n, share) + y.shape[1:], y.dtype),
            pltpu.SemaphoreType.DMA((n - 1,)),
            pltpu.SemaphoreType.DMA((n,)),
            pltpu.SemaphoreType.DMA(()),
        ],
        compiler_params=pltpu.CompilerParams(collective_id=collective, has_side_effects=True),
    )(y, resid)


ln_eps = 1e-06


def contract(left, right, left_dim, right_dim):
    return lax.dot_general(
        left, right, (((left_dim,), (right_dim,)), ((), ())), preferred_element_type=jnp.float32
    )


def on_device(
    hidden_in, w_qkv, w_out, ln_gain, ln_bias, table, key_len, gold_block, gold_row, neg_blocks
):
    ment_rows, seq_len, width = hidden_in.shape
    local_cols = w_qkv.shape[2]
    local_heads = local_cols // HD
    own_blocks, block_rows = (table.shape[0], table.shape[1])
    score_scale = HD ** (-0.5)
    owner = lax.axis_index("ent")
    first_block = owner * own_blocks
    cls_rows = hidden_in[:, 0, :]
    w_query = w_qkv[:, 0, :]
    w_keyval = w_qkv[:, 1:, :].reshape(width, 2 * local_cols)
    query = jnp.dot(cls_rows, w_query, preferred_element_type=jnp.float32).astype(jnp.bfloat16)
    keyval = jnp.dot(
        hidden_in.reshape(ment_rows * seq_len, width), w_keyval, preferred_element_type=jnp.float32
    )
    keyval = keyval.astype(jnp.bfloat16).reshape(ment_rows, seq_len, 2, local_heads, HD)
    key_heads = keyval[:, :, 0]
    value_heads = keyval[:, :, 1]
    query_heads = query.reshape(ment_rows, local_heads, HD)
    attention_scores = (
        jnp.einsum("ybn,yqbn->ybq", query_heads, key_heads, preferred_element_type=jnp.float32)
        * score_scale
    )
    valid = (jnp.arange(seq_len, dtype=jnp.int32)[None, :] < key_len[:, None]).astype(jnp.float32)
    expo = jnp.exp(attention_scores) * valid[:, None, :]
    probs = expo / jnp.sum(expo, axis=-1, keepdims=True)
    probability_half = probs.astype(jnp.bfloat16)
    context_rows = jnp.einsum(
        "qjp,qpjb->qjb", probability_half, value_heads, preferred_element_type=jnp.float32
    )
    context_rows = context_rows.reshape(ment_rows, local_cols).astype(jnp.bfloat16)
    attn_part = jnp.dot(context_rows, w_out, preferred_element_type=jnp.float32)
    local_block = gold_block - first_block
    owned = (local_block >= 0) & (local_block < own_blocks)
    safe_block = jnp.clip(local_block, 0, own_blocks - 1)
    flat_table = table.reshape(own_blocks * block_rows, width)
    picked = flat_table[safe_block * block_rows + gold_row]
    picked = jnp.where(owned[:, None], picked.astype(jnp.float32), 0.0)
    both = peer_sum(
        jnp.concatenate([attn_part.astype(jnp.bfloat16), picked.astype(jnp.bfloat16)], axis=0), 0
    )
    attn_out, gold_sum = both[:ment_rows], both[ment_rows:]
    golds = gold_sum.astype(jnp.bfloat16)
    resid = cls_rows.astype(jnp.float32) + attn_out
    centre = resid - jnp.mean(resid, axis=-1, keepdims=True)
    rstd = lax.rsqrt(jnp.mean(centre * centre, axis=-1, keepdims=True) + ln_eps)
    normed = centre * rstd
    embed = (normed * ln_gain + ln_bias).astype(jnp.bfloat16)
    inbatch = contract(embed, golds, 1, 1)
    negscore = contract(embed, flat_table, 1, 1)
    block_ids = first_block + jnp.arange(own_blocks, dtype=jnp.int32)
    listed = jnp.any(neg_blocks[0][:, None] == block_ids[None, :], axis=0).astype(jnp.float32)
    row_mask = jnp.repeat(listed, block_rows)
    neg_part = jnp.sum(jnp.exp(negscore) * row_mask[None, :], axis=1)
    neg_total = peer_sum(jnp.pad(neg_part.reshape(1, ment_rows), ((0, 7), (0, 0))), 1)[0]
    lse = jnp.log(jnp.sum(jnp.exp(inbatch), axis=1) + neg_total)
    eye = jnp.eye(ment_rows, dtype=jnp.float32)
    w_inb = (jnp.exp(inbatch - lse[:, None]) - eye).astype(jnp.bfloat16)
    w_neg = (jnp.exp(negscore - lse[:, None]) * row_mask[None, :]).astype(jnp.bfloat16)
    embed_part = jnp.dot(w_neg, flat_table, preferred_element_type=jnp.float32)
    d_embed = jnp.dot(w_inb, golds, preferred_element_type=jnp.float32) + peer_sum(
        embed_part.astype(jnp.bfloat16), 2
    )
    ln_terms = jnp.stack([jnp.sum(d_embed * normed, axis=0), jnp.sum(d_embed, axis=0)])
    upper = d_embed * ln_gain
    d_resid = rstd * (
        upper
        - jnp.mean(upper, axis=-1, keepdims=True)
        - normed * jnp.mean(upper * normed, axis=-1, keepdims=True)
    )
    d_resid_bf = d_resid.astype(jnp.bfloat16)
    wo_term = contract(context_rows, d_resid_bf, 0, 0)
    d_context = contract(d_resid_bf, w_out, 1, 1).astype(jnp.bfloat16)
    context_head_gradient = d_context.reshape(ment_rows, local_heads, HD)
    probability_gradient = jnp.einsum(
        "ybn,yqbn->ybq", context_head_gradient, value_heads, preferred_element_type=jnp.float32
    )
    score_gradient = probs * (
        probability_gradient - jnp.sum(probs * probability_gradient, axis=-1, keepdims=True)
    )
    query_gradient = (
        jnp.einsum("qjp,qpjb->qjb", score_gradient, key_heads, preferred_element_type=jnp.float32)
        * score_scale
    )
    query_gradient = query_gradient.reshape(ment_rows, local_cols).astype(jnp.bfloat16)
    key_gradient = (
        jnp.einsum("ryk,ryo->rkyo", score_gradient, query_heads, preferred_element_type=jnp.float32)
        * score_scale
    )
    value_gradient = jnp.einsum(
        "ryk,ryo->rkyo", probability_half, context_head_gradient, preferred_element_type=jnp.float32
    )
    d_keyval = (
        jnp.stack([key_gradient, value_gradient], axis=2)
        .reshape(ment_rows, seq_len, 2 * local_cols)
        .astype(jnp.bfloat16)
    )
    flat_grad = d_keyval.reshape(ment_rows * seq_len, 2 * local_cols)
    count = lax.axis_size("ment") * (width // lax.axis_size("ment"))
    kv_term = contract(hidden_in.reshape(ment_rows * seq_len, count), flat_grad, 0, 0)
    query_term = contract(hidden_in[:, 0, :], query_gradient, 0, 0)
    qkv_term = jnp.concatenate(
        [query_term[:, None, :], kv_term.reshape(count, 2, local_cols)], axis=1
    )
    share = ment_rows // lax.axis_size("ent")
    grad_part = d_keyval.reshape(share * lax.axis_size("ent") * seq_len, 2 * local_cols)
    token_term = contract(grad_part, w_keyval, 1, 1).reshape(
        share * lax.axis_size("ent"), seq_len, width
    )
    resid_mine = lax.dynamic_slice_in_dim(d_resid, owner * share, share, 0)
    grad_hidden = peer_scatter(
        token_term.at[:, 0, :].add(contract(query_gradient, w_query, 1, 1)).astype(jnp.bfloat16),
        resid_mine,
        3,
    )
    gold_terms = contract(w_inb, embed, 0, 0)
    weight_blocks = w_neg.reshape(ment_rows, own_blocks, block_rows)
    count = lax.axis_size("ment") * (block_rows // lax.axis_size("ment"))
    neg_term = jnp.einsum("mbr,md->rbd", weight_blocks, embed, preferred_element_type=jnp.float32)
    inside = owned & (gold_row >= 0) & (gold_row < count)
    row_slot = jnp.where(inside, gold_row, count)
    table_term = neg_term.at[row_slot, safe_block].add(gold_terms, mode="drop")
    parts = lax.axis_size("ment")
    qkv_rows = width // parts
    wo_cols = width // parts
    slab = own_blocks * width
    table_piece = table_term.reshape(parts, -1, own_blocks, width)
    rows_piece = jnp.concatenate(
        [qkv_term.reshape(width, 3 * local_cols), wo_term.T], axis=1
    ).reshape(parts, -1, own_blocks, width)
    ln_flat = ln_terms.T.reshape(parts, -1)
    ln_piece = jnp.pad(ln_flat, ((0, 0), (0, -ln_flat.shape[1] % slab))).reshape(
        parts, -1, own_blocks, width
    )
    pieces = [table_piece, rows_piece, ln_piece]
    counts = [piece.shape[1] for piece in pieces]
    merged = lax.psum_scatter(
        jnp.concatenate(pieces, axis=1).reshape(-1, own_blocks, width),
        "ment",
        scatter_dimension=0,
        tiled=True,
    )
    merged = lax.optimization_barrier(merged)
    table_sum = merged[: counts[0]]
    rows_sum = merged[counts[0] : counts[0] + counts[1]].reshape(qkv_rows, -1)
    ln_sum = merged[counts[0] + counts[1] :].reshape(-1)[: ln_flat.shape[1]]
    grad_table = table_sum.transpose(1, 0, 2)
    grad_qkv = rows_sum[:, : 3 * local_cols].reshape(qkv_rows, 3, local_cols)
    grad_wo = rows_sum[:, 3 * local_cols :].T
    grad_ln = ln_sum.reshape(wo_cols, 2).T
    return (grad_hidden, grad_qkv, grad_wo, grad_ln, grad_table)


def solution(mesh):
    placed = (
        P("ment", None, None),
        P(None, None, "ent"),
        P("ent", None),
        P(),
        P(),
        P("ent", None, None),
        P("ment"),
        P("ment"),
        P("ment"),
        P("ment", None),
    )
    return jax.shard_map(
        on_device,
        mesh=mesh,
        in_specs=placed,
        out_specs=(
            P(("ment", "ent"), None, None),
            P("ment", None, "ent"),
            P("ent", "ment"),
            P(None, "ment"),
            P("ent", "ment", None),
        ),
        check_vma=False,
    )
```

```python
import functools

import jax
import jax.numpy as jnp
from jax import lax
from jax.experimental import pallas as pl
from jax.experimental.pallas import tpu as pltpu
from jax.sharding import PartitionSpec as P

HD = 64
MESH = pl.DeviceIdType.MESH


def _greet_peers(row, me, n):
    barrier = pltpu.get_barrier_semaphore()
    for k in range(1, n):
        pl.semaphore_signal(
            barrier, inc=1, device_id=(row, lax.rem(me + k, n)), device_id_type=MESH
        )
    pl.semaphore_wait(barrier, n - 1)


def _peer_sum_kernel(n, x_ref, out_ref, recv, send_sem, recv_sem, own_sem):
    row = lax.axis_index("ment")
    me = lax.axis_index("ent")
    _greet_peers(row, me, n)
    sends = []
    for k in range(1, n):
        copy = pltpu.make_async_remote_copy(
            src_ref=x_ref,
            dst_ref=recv.at[me],
            send_sem=send_sem.at[k - 1],
            recv_sem=recv_sem.at[me],
            device_id=(row, lax.rem(me + k, n)),
            device_id_type=MESH,
        )
        copy.start()
        sends.append(copy)
    own = pltpu.make_async_copy(x_ref, recv.at[me], own_sem)
    own.start()
    for k in range(1, n):
        source = lax.rem(me + n - k, n)
        pltpu.make_async_remote_copy(
            src_ref=x_ref,
            dst_ref=recv.at[source],
            send_sem=send_sem.at[k - 1],
            recv_sem=recv_sem.at[source],
            device_id=(row, source),
            device_id_type=MESH,
        ).wait_recv()
    own.wait()
    for copy in sends:
        copy.wait_send()
    total = recv[0].astype(jnp.float32)
    for s in range(1, n):
        total = total + recv[s].astype(jnp.float32)
    out_ref[...] = total


def peer_sum(x, collective):
    n = lax.axis_size("ent")
    return pl.pallas_call(
        functools.partial(_peer_sum_kernel, n),
        out_shape=jax.ShapeDtypeStruct(x.shape, jnp.float32),
        in_specs=[pl.BlockSpec(memory_space=pltpu.VMEM)],
        out_specs=pl.BlockSpec(memory_space=pltpu.VMEM),
        scratch_shapes=[
            pltpu.VMEM((n,) + x.shape, x.dtype),
            pltpu.SemaphoreType.DMA((n - 1,)),
            pltpu.SemaphoreType.DMA((n,)),
            pltpu.SemaphoreType.DMA(()),
        ],
        compiler_params=pltpu.CompilerParams(collective_id=collective, has_side_effects=True),
    )(x)


def _peer_scatter_kernel(n, y_ref, resid_ref, out_ref, recv, send_sem, recv_sem, own_sem):
    row = lax.axis_index("ment")
    me = lax.axis_index("ent")
    share = out_ref.shape[0]
    _greet_peers(row, me, n)
    sends = []
    for k in range(1, n):
        target = lax.rem(me + k, n)
        copy = pltpu.make_async_remote_copy(
            src_ref=y_ref.at[pl.ds(target * share, share)],
            dst_ref=recv.at[me],
            send_sem=send_sem.at[k - 1],
            recv_sem=recv_sem.at[me],
            device_id=(row, target),
            device_id_type=MESH,
        )
        copy.start()
        sends.append(copy)
    own = pltpu.make_async_copy(y_ref.at[pl.ds(me * share, share)], recv.at[me], own_sem)
    own.start()
    for k in range(1, n):
        source = lax.rem(me + n - k, n)
        pltpu.make_async_remote_copy(
            src_ref=y_ref.at[pl.ds(0, share)],
            dst_ref=recv.at[source],
            send_sem=send_sem.at[k - 1],
            recv_sem=recv_sem.at[source],
            device_id=(row, source),
            device_id_type=MESH,
        ).wait_recv()
    own.wait()
    for copy in sends:
        copy.wait_send()
    first = lax.broadcasted_iota(jnp.int32, out_ref.shape[1:], 0) == 0

    def one_mention(i, carry):
        total = recv[0, i].astype(jnp.float32)
        for s in range(1, n):
            total = total + recv[s, i].astype(jnp.float32)
        total = total + jnp.where(first, resid_ref[pl.ds(i, 1), :], 0.0)
        out_ref[i] = total.astype(out_ref.dtype)
        return carry

    lax.fori_loop(0, share, one_mention, 0)


def peer_scatter(y, resid, collective):
    n = lax.axis_size("ent")
    share = y.shape[0] // n
    return pl.pallas_call(
        functools.partial(_peer_scatter_kernel, n),
        out_shape=jax.ShapeDtypeStruct((share,) + y.shape[1:], jnp.bfloat16),
        in_specs=[pl.BlockSpec(memory_space=pltpu.VMEM)] * 2,
        out_specs=pl.BlockSpec(memory_space=pltpu.VMEM),
        scratch_shapes=[
            pltpu.VMEM((n, share) + y.shape[1:], y.dtype),
            pltpu.SemaphoreType.DMA((n - 1,)),
            pltpu.SemaphoreType.DMA((n,)),
            pltpu.SemaphoreType.DMA(()),
        ],
        compiler_params=pltpu.CompilerParams(collective_id=collective, has_side_effects=True),
    )(y, resid)


ln_eps = 1e-06


def contract(left, right, left_dim, right_dim):
    return lax.dot_general(
        left, right, (((left_dim,), (right_dim,)), ((), ())), preferred_element_type=jnp.float32
    )


def on_device(
    hidden_in, w_qkv, w_out, ln_gain, ln_bias, table, key_len, gold_block, gold_row, neg_blocks
):
    ment_rows, seq_len, width = hidden_in.shape
    local_cols = w_qkv.shape[2]
    local_heads = local_cols // HD
    own_blocks, block_rows = (table.shape[0], table.shape[1])
    score_scale = HD ** (-0.5)
    owner = lax.axis_index("ent")
    first_block = owner * own_blocks
    cls_rows = hidden_in[:, 0, :]
    w_query = w_qkv[:, 0, :]
    w_keyval = w_qkv[:, 1:, :].reshape(width, 2 * local_cols)
    query = jnp.dot(cls_rows, w_query, preferred_element_type=jnp.float32).astype(jnp.bfloat16)
    keyval = jnp.dot(
        hidden_in.reshape(ment_rows * seq_len, width), w_keyval, preferred_element_type=jnp.float32
    )
    keyval = keyval.astype(jnp.bfloat16).reshape(ment_rows, seq_len, 2, local_heads, HD)
    key_heads = keyval[:, :, 0]
    value_heads = keyval[:, :, 1]
    query_heads = query.reshape(ment_rows, local_heads, HD)
    attention_scores = (
        jnp.einsum("ybn,yqbn->ybq", query_heads, key_heads, preferred_element_type=jnp.float32)
        * score_scale
    )
    valid = (jnp.arange(seq_len, dtype=jnp.int32)[None, :] < key_len[:, None]).astype(jnp.float32)
    expo = jnp.exp(attention_scores) * valid[:, None, :]
    probs = expo / jnp.sum(expo, axis=-1, keepdims=True)
    probability_half = probs.astype(jnp.bfloat16)
    context_rows = jnp.einsum(
        "qjp,qpjb->qjb", probability_half, value_heads, preferred_element_type=jnp.float32
    )
    context_rows = context_rows.reshape(ment_rows, local_cols).astype(jnp.bfloat16)
    attn_part = jnp.dot(context_rows, w_out, preferred_element_type=jnp.float32)
    local_block = gold_block - first_block
    owned = (local_block >= 0) & (local_block < own_blocks)
    safe_block = jnp.clip(local_block, 0, own_blocks - 1)
    flat_table = table.reshape(own_blocks * block_rows, width)
    picked = flat_table[safe_block * block_rows + gold_row]
    picked = jnp.where(owned[:, None], picked.astype(jnp.float32), 0.0)
    both = peer_sum(
        jnp.concatenate([attn_part.astype(jnp.bfloat16), picked.astype(jnp.bfloat16)], axis=0), 0
    )
    attn_out, gold_sum = both[:ment_rows], both[ment_rows:]
    golds = gold_sum.astype(jnp.bfloat16)
    resid = cls_rows.astype(jnp.float32) + attn_out
    centre = resid - jnp.mean(resid, axis=-1, keepdims=True)
    rstd = lax.rsqrt(jnp.mean(centre * centre, axis=-1, keepdims=True) + ln_eps)
    normed = centre * rstd
    embed = (normed * ln_gain + ln_bias).astype(jnp.bfloat16)
    inbatch = contract(embed, golds, 1, 1)
    negscore = contract(embed, flat_table, 1, 1)
    block_ids = first_block + jnp.arange(own_blocks, dtype=jnp.int32)
    listed = jnp.any(neg_blocks[0][:, None] == block_ids[None, :], axis=0).astype(jnp.float32)
    row_mask = jnp.repeat(listed, block_rows)
    neg_part = jnp.sum(jnp.exp(negscore) * row_mask[None, :], axis=1)
    neg_total = peer_sum(jnp.pad(neg_part.reshape(1, ment_rows), ((0, 7), (0, 0))), 1)[0]
    lse = jnp.log(jnp.sum(jnp.exp(inbatch), axis=1) + neg_total)
    eye = jnp.eye(ment_rows, dtype=jnp.float32)
    w_inb = (jnp.exp(inbatch - lse[:, None]) - eye).astype(jnp.bfloat16)
    w_neg = (jnp.exp(negscore - lse[:, None]) * row_mask[None, :]).astype(jnp.bfloat16)
    embed_part = jnp.dot(w_neg, flat_table, preferred_element_type=jnp.float32)
    d_embed = jnp.dot(w_inb, golds, preferred_element_type=jnp.float32) + peer_sum(
        embed_part.astype(jnp.bfloat16), 2
    )
    ln_terms = jnp.stack([jnp.sum(d_embed * normed, axis=0), jnp.sum(d_embed, axis=0)])
    upper = d_embed * ln_gain
    d_resid = rstd * (
        upper
        - jnp.mean(upper, axis=-1, keepdims=True)
        - normed * jnp.mean(upper * normed, axis=-1, keepdims=True)
    )
    d_resid_bf = d_resid.astype(jnp.bfloat16)
    d_context = contract(d_resid_bf, w_out, 1, 1).astype(jnp.bfloat16)
    context_head_gradient = d_context.reshape(ment_rows, local_heads, HD)
    probability_gradient = jnp.einsum(
        "ybn,yqbn->ybq", context_head_gradient, value_heads, preferred_element_type=jnp.float32
    )
    score_gradient = probs * (
        probability_gradient - jnp.sum(probs * probability_gradient, axis=-1, keepdims=True)
    )
    query_gradient = (
        jnp.einsum("qjp,qpjb->qjb", score_gradient, key_heads, preferred_element_type=jnp.float32)
        * score_scale
    )
    query_gradient = query_gradient.reshape(ment_rows, local_cols).astype(jnp.bfloat16)
    key_gradient = (
        jnp.einsum("ryk,ryo->rkyo", score_gradient, query_heads, preferred_element_type=jnp.float32)
        * score_scale
    )
    value_gradient = jnp.einsum(
        "ryk,ryo->rkyo", probability_half, context_head_gradient, preferred_element_type=jnp.float32
    )
    d_keyval = (
        jnp.stack([key_gradient, value_gradient], axis=2)
        .reshape(ment_rows, seq_len, 2 * local_cols)
        .astype(jnp.bfloat16)
    )
    flat_grad = d_keyval.reshape(ment_rows * seq_len, 2 * local_cols)
    count = lax.axis_size("ment") * (width // lax.axis_size("ment"))
    kv_term = contract(hidden_in.reshape(ment_rows * seq_len, count), flat_grad, 0, 0)
    query_term = contract(hidden_in[:, 0, :], query_gradient, 0, 0)
    share = ment_rows // lax.axis_size("ent")
    grad_part = d_keyval.reshape(share * lax.axis_size("ent") * seq_len, 2 * local_cols)
    token_term = contract(grad_part, w_keyval, 1, 1).reshape(
        share * lax.axis_size("ent"), seq_len, width
    )
    resid_mine = lax.dynamic_slice_in_dim(d_resid, owner * share, share, 0)
    grad_hidden = peer_scatter(
        token_term.at[:, 0, :].add(contract(query_gradient, w_query, 1, 1)).astype(jnp.bfloat16),
        resid_mine,
        3,
    )
    gold_terms = contract(w_inb, embed, 0, 0)
    neg_weights = (
        w_neg.reshape(ment_rows, own_blocks, block_rows).transpose(0, 2, 1).reshape(ment_rows, -1)
    )
    slot = gold_row * own_blocks + safe_block
    hit = (slot[:, None] == jnp.arange(block_rows * own_blocks)[None, :]) & owned[:, None]
    gold_add = lax.dot_general(
        hit.astype(jnp.float32),
        gold_terms,
        (((0,), (0,)), ((), ())),
        precision=lax.Precision.HIGHEST,
        preferred_element_type=jnp.float32,
    )
    table_term = contract(neg_weights, embed, 0, 0) + gold_add
    parts = lax.axis_size("ment")
    qkv_rows = width // parts
    wo_cols = width // parts
    slab = own_blocks * width
    table_piece = table_term.reshape(parts, -1, own_blocks, width)
    rows_piece = jnp.concatenate(
        [query_term, kv_term, contract(d_resid_bf, context_rows, 0, 0)], axis=1
    ).reshape(parts, -1, own_blocks, width)
    ln_flat = ln_terms.T.reshape(parts, -1)
    ln_piece = jnp.pad(ln_flat, ((0, 0), (0, -ln_flat.shape[1] % slab))).reshape(
        parts, -1, own_blocks, width
    )
    pieces = [table_piece, rows_piece, ln_piece]
    counts = [piece.shape[1] for piece in pieces]
    merged = lax.psum_scatter(
        jnp.concatenate(pieces, axis=1).reshape(-1, own_blocks, width),
        "ment",
        scatter_dimension=0,
        tiled=True,
    )
    merged = lax.optimization_barrier(merged)
    table_sum = merged[: counts[0]]
    rows_sum = merged[counts[0] : counts[0] + counts[1]].reshape(qkv_rows, -1)
    ln_sum = merged[counts[0] + counts[1] :].reshape(-1)[: ln_flat.shape[1]]
    grad_table = table_sum.transpose(1, 0, 2)
    grad_qkv = rows_sum[:, : 3 * local_cols].reshape(qkv_rows, 3, local_cols)
    grad_wo = rows_sum[:, 3 * local_cols :].T
    grad_ln = ln_sum.reshape(wo_cols, 2).T
    return (grad_hidden, grad_qkv, grad_wo, grad_ln, grad_table)


def solution(mesh):
    placed = (
        P("ment", None, None),
        P(None, None, "ent"),
        P("ent", None),
        P(),
        P(),
        P("ent", None, None),
        P("ment"),
        P("ment"),
        P("ment"),
        P("ment", None),
    )
    return jax.shard_map(
        on_device,
        mesh=mesh,
        in_specs=placed,
        out_specs=(
            P(("ment", "ent"), None, None),
            P("ment", None, "ent"),
            P("ent", "ment"),
            P(None, "ment"),
            P("ent", "ment", None),
        ),
        check_vma=False,
    )
```

```python
import functools

import jax
import jax.numpy as jnp
from jax import lax
from jax.experimental import pallas as pl
from jax.experimental.pallas import tpu as pltpu
from jax.sharding import PartitionSpec as P

HD = 64
MESH = pl.DeviceIdType.MESH


def _greet_peers(row, me, n):
    barrier = pltpu.get_barrier_semaphore()
    for k in range(1, n):
        pl.semaphore_signal(
            barrier, inc=1, device_id=(row, lax.rem(me + k, n)), device_id_type=MESH
        )
    pl.semaphore_wait(barrier, n - 1)


def _peer_sum_kernel(n, x_ref, out_ref, recv, send_sem, recv_sem, own_sem):
    row = lax.axis_index("ment")
    me = lax.axis_index("ent")
    _greet_peers(row, me, n)
    sends = []
    for k in range(1, n):
        copy = pltpu.make_async_remote_copy(
            src_ref=x_ref,
            dst_ref=recv.at[me],
            send_sem=send_sem.at[k - 1],
            recv_sem=recv_sem.at[me],
            device_id=(row, lax.rem(me + k, n)),
            device_id_type=MESH,
        )
        copy.start()
        sends.append(copy)
    own = pltpu.make_async_copy(x_ref, recv.at[me], own_sem)
    own.start()
    for k in range(1, n):
        source = lax.rem(me + n - k, n)
        pltpu.make_async_remote_copy(
            src_ref=x_ref,
            dst_ref=recv.at[source],
            send_sem=send_sem.at[k - 1],
            recv_sem=recv_sem.at[source],
            device_id=(row, source),
            device_id_type=MESH,
        ).wait_recv()
    own.wait()
    for copy in sends:
        copy.wait_send()
    total = recv[0].astype(jnp.float32)
    for s in range(1, n):
        total = total + recv[s].astype(jnp.float32)
    out_ref[...] = total


def peer_sum(x, collective):
    n = lax.axis_size("ent")
    return pl.pallas_call(
        functools.partial(_peer_sum_kernel, n),
        out_shape=jax.ShapeDtypeStruct(x.shape, jnp.float32),
        in_specs=[pl.BlockSpec(memory_space=pltpu.VMEM)],
        out_specs=pl.BlockSpec(memory_space=pltpu.VMEM),
        scratch_shapes=[
            pltpu.VMEM((n,) + x.shape, x.dtype),
            pltpu.SemaphoreType.DMA((n - 1,)),
            pltpu.SemaphoreType.DMA((n,)),
            pltpu.SemaphoreType.DMA(()),
        ],
        compiler_params=pltpu.CompilerParams(collective_id=collective, has_side_effects=True),
    )(x)


def _peer_scatter_kernel(n, y_ref, resid_ref, out_ref, recv, send_sem, recv_sem, own_sem):
    row = lax.axis_index("ment")
    me = lax.axis_index("ent")
    share = out_ref.shape[0]
    _greet_peers(row, me, n)
    sends = []
    for k in range(1, n):
        target = lax.rem(me + k, n)
        copy = pltpu.make_async_remote_copy(
            src_ref=y_ref.at[pl.ds(target * share, share)],
            dst_ref=recv.at[me],
            send_sem=send_sem.at[k - 1],
            recv_sem=recv_sem.at[me],
            device_id=(row, target),
            device_id_type=MESH,
        )
        copy.start()
        sends.append(copy)
    own = pltpu.make_async_copy(y_ref.at[pl.ds(me * share, share)], recv.at[me], own_sem)
    own.start()
    for k in range(1, n):
        source = lax.rem(me + n - k, n)
        pltpu.make_async_remote_copy(
            src_ref=y_ref.at[pl.ds(0, share)],
            dst_ref=recv.at[source],
            send_sem=send_sem.at[k - 1],
            recv_sem=recv_sem.at[source],
            device_id=(row, source),
            device_id_type=MESH,
        ).wait_recv()
    own.wait()
    for copy in sends:
        copy.wait_send()
    first = lax.broadcasted_iota(jnp.int32, out_ref.shape[1:], 0) == 0

    def one_mention(i, carry):
        total = recv[0, i].astype(jnp.float32)
        for s in range(1, n):
            total = total + recv[s, i].astype(jnp.float32)
        total = total + jnp.where(first, resid_ref[pl.ds(i, 1), :], 0.0)
        out_ref[i] = total.astype(out_ref.dtype)
        return carry

    lax.fori_loop(0, share, one_mention, 0)


def peer_scatter(y, resid, collective):
    n = lax.axis_size("ent")
    share = y.shape[0] // n
    return pl.pallas_call(
        functools.partial(_peer_scatter_kernel, n),
        out_shape=jax.ShapeDtypeStruct((share,) + y.shape[1:], jnp.bfloat16),
        in_specs=[pl.BlockSpec(memory_space=pltpu.VMEM)] * 2,
        out_specs=pl.BlockSpec(memory_space=pltpu.VMEM),
        scratch_shapes=[
            pltpu.VMEM((n, share) + y.shape[1:], y.dtype),
            pltpu.SemaphoreType.DMA((n - 1,)),
            pltpu.SemaphoreType.DMA((n,)),
            pltpu.SemaphoreType.DMA(()),
        ],
        compiler_params=pltpu.CompilerParams(collective_id=collective, has_side_effects=True),
    )(y, resid)


ln_eps = 1e-06


def contract(left, right, left_dim, right_dim):
    return lax.dot_general(
        left, right, (((left_dim,), (right_dim,)), ((), ())), preferred_element_type=jnp.float32
    )


def on_device(
    hidden_in, w_qkv, w_out, ln_gain, ln_bias, table, key_len, gold_block, gold_row, neg_blocks
):
    ment_rows, seq_len, width = hidden_in.shape
    local_cols = w_qkv.shape[2]
    local_heads = local_cols // HD
    own_blocks, block_rows = (table.shape[0], table.shape[1])
    score_scale = HD ** (-0.5)
    owner = lax.axis_index("ent")
    first_block = owner * own_blocks
    cls_rows = hidden_in[:, 0, :]
    w_query = w_qkv[:, 0, :]
    w_keyval = w_qkv[:, 1:, :].reshape(width, 2 * local_cols)
    query = jnp.dot(cls_rows, w_query, preferred_element_type=jnp.float32).astype(jnp.bfloat16)
    keyval = jnp.dot(
        hidden_in.reshape(ment_rows * seq_len, width), w_keyval, preferred_element_type=jnp.float32
    )
    keyval = keyval.astype(jnp.bfloat16).reshape(ment_rows, seq_len, 2, local_heads, HD)
    key_heads = keyval[:, :, 0]
    value_heads = keyval[:, :, 1]
    query_heads = query.reshape(ment_rows, local_heads, HD)
    attention_scores = (
        jnp.einsum("ybn,yqbn->ybq", query_heads, key_heads, preferred_element_type=jnp.float32)
        * score_scale
    )
    valid = (jnp.arange(seq_len, dtype=jnp.int32)[None, :] < key_len[:, None]).astype(jnp.float32)
    expo = jnp.exp(attention_scores) * valid[:, None, :]
    probs = expo / jnp.sum(expo, axis=-1, keepdims=True)
    probability_half = probs.astype(jnp.bfloat16)
    context_rows = jnp.einsum(
        "qjp,qpjb->qjb", probability_half, value_heads, preferred_element_type=jnp.float32
    )
    context_rows = context_rows.reshape(ment_rows, local_cols).astype(jnp.bfloat16)
    attn_part = jnp.dot(context_rows, w_out, preferred_element_type=jnp.float32)
    local_block = gold_block - first_block
    owned = (local_block >= 0) & (local_block < own_blocks)
    safe_block = jnp.clip(local_block, 0, own_blocks - 1)
    flat_table = table.reshape(own_blocks * block_rows, width)
    picked = flat_table[safe_block * block_rows + gold_row]
    picked = jnp.where(owned[:, None], picked.astype(jnp.float32), 0.0)
    both = peer_sum(
        jnp.concatenate([attn_part.astype(jnp.bfloat16), picked.astype(jnp.bfloat16)], axis=0), 0
    )
    attn_out, gold_sum = both[:ment_rows], both[ment_rows:]
    golds = gold_sum.astype(jnp.bfloat16)
    resid = cls_rows.astype(jnp.float32) + attn_out
    centre = resid - jnp.mean(resid, axis=-1, keepdims=True)
    rstd = lax.rsqrt(jnp.mean(centre * centre, axis=-1, keepdims=True) + ln_eps)
    normed = centre * rstd
    embed = (normed * ln_gain + ln_bias).astype(jnp.bfloat16)
    inbatch = contract(embed, golds, 1, 1)
    negscore = contract(embed, flat_table, 1, 1)
    block_ids = first_block + jnp.arange(own_blocks, dtype=jnp.int32)
    listed = jnp.any(neg_blocks[0][:, None] == block_ids[None, :], axis=0).astype(jnp.float32)
    row_mask = jnp.repeat(listed, block_rows)
    neg_part = jnp.sum(jnp.exp(negscore) * row_mask[None, :], axis=1)
    neg_total = peer_sum(jnp.pad(neg_part.reshape(1, ment_rows), ((0, 7), (0, 0))), 1)[0]
    lse = jnp.log(jnp.sum(jnp.exp(inbatch), axis=1) + neg_total)
    eye = jnp.eye(ment_rows, dtype=jnp.float32)
    w_inb = (jnp.exp(inbatch - lse[:, None]) - eye).astype(jnp.bfloat16)
    w_neg = (jnp.exp(negscore - lse[:, None]) * row_mask[None, :]).astype(jnp.bfloat16)
    embed_part = jnp.dot(w_neg, flat_table, preferred_element_type=jnp.float32)
    d_embed = jnp.dot(w_inb, golds, preferred_element_type=jnp.float32) + peer_sum(
        embed_part.astype(jnp.bfloat16), 2
    )
    ln_terms = jnp.stack([jnp.sum(d_embed * normed, axis=0), jnp.sum(d_embed, axis=0)])
    upper = d_embed * ln_gain
    d_resid = rstd * (
        upper
        - jnp.mean(upper, axis=-1, keepdims=True)
        - normed * jnp.mean(upper * normed, axis=-1, keepdims=True)
    )
    d_resid_bf = d_resid.astype(jnp.bfloat16)
    d_context = contract(d_resid_bf, w_out, 1, 1).astype(jnp.bfloat16)
    context_head_gradient = d_context.reshape(ment_rows, local_heads, HD)
    probability_gradient = jnp.einsum(
        "ybn,yqbn->ybq", context_head_gradient, value_heads, preferred_element_type=jnp.float32
    )
    score_gradient = probs * (
        probability_gradient - jnp.sum(probs * probability_gradient, axis=-1, keepdims=True)
    )
    query_gradient = (
        jnp.einsum("qjp,qpjb->qjb", score_gradient, key_heads, preferred_element_type=jnp.float32)
        * score_scale
    )
    query_gradient = query_gradient.reshape(ment_rows, local_cols).astype(jnp.bfloat16)
    key_gradient = (
        jnp.einsum("ryk,ryo->rkyo", score_gradient, query_heads, preferred_element_type=jnp.float32)
        * score_scale
    )
    value_gradient = jnp.einsum(
        "ryk,ryo->rkyo", probability_half, context_head_gradient, preferred_element_type=jnp.float32
    )
    d_keyval = jnp.stack([key_gradient, value_gradient], axis=2).astype(jnp.bfloat16)
    kv_term = lax.dot_general(
        hidden_in, d_keyval, (((0, 1), (0, 1)), ((), ())), preferred_element_type=jnp.float32
    ).reshape(width, 2 * local_cols)
    query_term = contract(hidden_in[:, 0, :], query_gradient, 0, 0)
    share = ment_rows // lax.axis_size("ent")
    token_term = lax.dot_general(
        d_keyval,
        w_keyval.reshape(width, 2, local_heads, HD),
        (((2, 3, 4), (1, 2, 3)), ((), ())),
        preferred_element_type=jnp.float32,
    )
    resid_mine = lax.dynamic_slice_in_dim(d_resid, owner * share, share, 0)
    grad_hidden = peer_scatter(
        token_term.at[:, 0, :].add(contract(query_gradient, w_query, 1, 1)).astype(jnp.bfloat16),
        resid_mine,
        3,
    )
    gold_terms = contract(w_inb, embed, 0, 0)
    neg_weights = (
        w_neg.reshape(ment_rows, own_blocks, block_rows).transpose(0, 2, 1).reshape(ment_rows, -1)
    )
    slot = gold_row * own_blocks + safe_block
    hit = (slot[:, None] == jnp.arange(block_rows * own_blocks)[None, :]) & owned[:, None]
    gold_add = lax.dot_general(
        hit.astype(jnp.float32),
        gold_terms,
        (((0,), (0,)), ((), ())),
        precision=lax.Precision.HIGHEST,
        preferred_element_type=jnp.float32,
    )
    table_term = contract(neg_weights, embed, 0, 0) + gold_add
    parts = lax.axis_size("ment")
    qkv_rows = width // parts
    wo_cols = width // parts
    slab = own_blocks * width
    table_piece = table_term.reshape(parts, -1, own_blocks, width)
    rows_piece = jnp.concatenate(
        [query_term, kv_term, contract(d_resid_bf, context_rows, 0, 0)], axis=1
    ).reshape(parts, -1, own_blocks, width)
    ln_flat = ln_terms.T.reshape(parts, -1)
    ln_piece = jnp.pad(ln_flat, ((0, 0), (0, -ln_flat.shape[1] % slab))).reshape(
        parts, -1, own_blocks, width
    )
    pieces = [table_piece, rows_piece, ln_piece]
    counts = [piece.shape[1] for piece in pieces]
    merged = lax.psum_scatter(
        jnp.concatenate(pieces, axis=1).reshape(-1, own_blocks, width),
        "ment",
        scatter_dimension=0,
        tiled=True,
    )
    merged = lax.optimization_barrier(merged)
    table_sum = merged[: counts[0]]
    rows_sum = merged[counts[0] : counts[0] + counts[1]].reshape(qkv_rows, -1)
    ln_sum = merged[counts[0] + counts[1] :].reshape(-1)[: ln_flat.shape[1]]
    grad_table = table_sum.transpose(1, 0, 2)
    grad_qkv = rows_sum[:, : 3 * local_cols].reshape(qkv_rows, 3, local_cols)
    grad_wo = rows_sum[:, 3 * local_cols :].T
    grad_ln = ln_sum.reshape(wo_cols, 2).T
    return (grad_hidden, grad_qkv, grad_wo, grad_ln, grad_table)


def solution(mesh):
    placed = (
        P("ment", None, None),
        P(None, None, "ent"),
        P("ent", None),
        P(),
        P(),
        P("ent", None, None),
        P("ment"),
        P("ment"),
        P("ment"),
        P("ment", None),
    )
    return jax.shard_map(
        on_device,
        mesh=mesh,
        in_specs=placed,
        out_specs=(
            P(("ment", "ent"), None, None),
            P("ment", None, "ent"),
            P("ent", "ment"),
            P(None, "ment"),
            P("ent", "ment", None),
        ),
        check_vma=False,
    )
```

```python
import functools

import jax
import jax.numpy as jnp
from jax import lax
from jax.experimental import pallas as pl
from jax.experimental.pallas import tpu as pltpu
from jax.sharding import PartitionSpec as P

HD = 64
MESH = pl.DeviceIdType.MESH


def _greet_peers(row, me, n):
    barrier = pltpu.get_barrier_semaphore()
    for k in range(1, n):
        pl.semaphore_signal(
            barrier, inc=1, device_id=(row, lax.rem(me + k, n)), device_id_type=MESH
        )
    pl.semaphore_wait(barrier, n - 1)


def _peer_sum_kernel(n, x_ref, out_ref, recv, send_sem, recv_sem, own_sem):
    row = lax.axis_index("ment")
    me = lax.axis_index("ent")
    _greet_peers(row, me, n)
    sends = []
    for k in range(1, n):
        copy = pltpu.make_async_remote_copy(
            src_ref=x_ref,
            dst_ref=recv.at[me],
            send_sem=send_sem.at[k - 1],
            recv_sem=recv_sem.at[me],
            device_id=(row, lax.rem(me + k, n)),
            device_id_type=MESH,
        )
        copy.start()
        sends.append(copy)
    own = pltpu.make_async_copy(x_ref, recv.at[me], own_sem)
    own.start()
    for k in range(1, n):
        source = lax.rem(me + n - k, n)
        pltpu.make_async_remote_copy(
            src_ref=x_ref,
            dst_ref=recv.at[source],
            send_sem=send_sem.at[k - 1],
            recv_sem=recv_sem.at[source],
            device_id=(row, source),
            device_id_type=MESH,
        ).wait_recv()
    own.wait()
    for copy in sends:
        copy.wait_send()
    total = recv[0].astype(jnp.float32)
    for s in range(1, n):
        total = total + recv[s].astype(jnp.float32)
    out_ref[...] = total


def peer_sum(x, collective):
    n = lax.axis_size("ent")
    return pl.pallas_call(
        functools.partial(_peer_sum_kernel, n),
        out_shape=jax.ShapeDtypeStruct(x.shape, jnp.float32),
        in_specs=[pl.BlockSpec(memory_space=pltpu.VMEM)],
        out_specs=pl.BlockSpec(memory_space=pltpu.VMEM),
        scratch_shapes=[
            pltpu.VMEM((n,) + x.shape, x.dtype),
            pltpu.SemaphoreType.DMA((n - 1,)),
            pltpu.SemaphoreType.DMA((n,)),
            pltpu.SemaphoreType.DMA(()),
        ],
        compiler_params=pltpu.CompilerParams(collective_id=collective, has_side_effects=True),
    )(x)


def _peer_scatter_kernel(n, y_ref, resid_ref, out_ref, recv, send_sem, recv_sem, own_sem):
    row = lax.axis_index("ment")
    me = lax.axis_index("ent")
    share = out_ref.shape[0]
    _greet_peers(row, me, n)
    sends = []
    for k in range(1, n):
        target = lax.rem(me + k, n)
        copy = pltpu.make_async_remote_copy(
            src_ref=y_ref.at[pl.ds(target * share, share)],
            dst_ref=recv.at[me],
            send_sem=send_sem.at[k - 1],
            recv_sem=recv_sem.at[me],
            device_id=(row, target),
            device_id_type=MESH,
        )
        copy.start()
        sends.append(copy)
    own = pltpu.make_async_copy(y_ref.at[pl.ds(me * share, share)], recv.at[me], own_sem)
    own.start()
    for k in range(1, n):
        source = lax.rem(me + n - k, n)
        pltpu.make_async_remote_copy(
            src_ref=y_ref.at[pl.ds(0, share)],
            dst_ref=recv.at[source],
            send_sem=send_sem.at[k - 1],
            recv_sem=recv_sem.at[source],
            device_id=(row, source),
            device_id_type=MESH,
        ).wait_recv()
    own.wait()
    for copy in sends:
        copy.wait_send()
    first = lax.broadcasted_iota(jnp.int32, out_ref.shape[1:], 0) == 0

    def one_mention(i, carry):
        total = recv[0, i].astype(jnp.float32)
        for s in range(1, n):
            total = total + recv[s, i].astype(jnp.float32)
        total = total + jnp.where(first, resid_ref[pl.ds(i, 1), :], 0.0)
        out_ref[i] = total.astype(out_ref.dtype)
        return carry

    lax.fori_loop(0, share, one_mention, 0)


def peer_scatter(y, resid, collective):
    n = lax.axis_size("ent")
    share = y.shape[0] // n
    return pl.pallas_call(
        functools.partial(_peer_scatter_kernel, n),
        out_shape=jax.ShapeDtypeStruct((share,) + y.shape[1:], jnp.bfloat16),
        in_specs=[pl.BlockSpec(memory_space=pltpu.VMEM)] * 2,
        out_specs=pl.BlockSpec(memory_space=pltpu.VMEM),
        scratch_shapes=[
            pltpu.VMEM((n, share) + y.shape[1:], y.dtype),
            pltpu.SemaphoreType.DMA((n - 1,)),
            pltpu.SemaphoreType.DMA((n,)),
            pltpu.SemaphoreType.DMA(()),
        ],
        compiler_params=pltpu.CompilerParams(collective_id=collective, has_side_effects=True),
    )(y, resid)


ln_eps = 1e-06


def contract(left, right, left_dim, right_dim):
    return lax.dot_general(
        left, right, (((left_dim,), (right_dim,)), ((), ())), preferred_element_type=jnp.float32
    )


def on_device(
    hidden_in, w_qkv, w_out, ln_gain, ln_bias, table, key_len, gold_block, gold_row, neg_blocks
):
    ment_rows, seq_len, width = hidden_in.shape
    local_cols = w_qkv.shape[2]
    local_heads = local_cols // HD
    own_blocks, block_rows = (table.shape[0], table.shape[1])
    score_scale = HD ** (-0.5)
    owner = lax.axis_index("ent")
    first_block = owner * own_blocks
    cls_rows = hidden_in[:, 0, :]
    w_query = w_qkv[:, 0, :]
    w_keyval = w_qkv[:, 1:, :].reshape(width, 2 * local_cols)
    query = jnp.dot(cls_rows, w_query, preferred_element_type=jnp.float32).astype(jnp.bfloat16)
    keyval = lax.dot_general(
        hidden_in,
        w_keyval.reshape(width, 2, local_heads, HD),
        (((2,), (0,)), ((), ())),
        preferred_element_type=jnp.float32,
    ).astype(jnp.bfloat16)
    key_heads = keyval[:, :, 0]
    value_heads = keyval[:, :, 1]
    query_heads = query.reshape(ment_rows, local_heads, HD)
    attention_scores = (
        jnp.einsum("ybn,yqbn->ybq", query_heads, key_heads, preferred_element_type=jnp.float32)
        * score_scale
    )
    valid = (jnp.arange(seq_len, dtype=jnp.int32)[None, :] < key_len[:, None]).astype(jnp.float32)
    expo = jnp.exp(attention_scores) * valid[:, None, :]
    probs = expo / jnp.sum(expo, axis=-1, keepdims=True)
    probability_half = probs.astype(jnp.bfloat16)
    context_rows = jnp.einsum(
        "qjp,qpjb->qjb", probability_half, value_heads, preferred_element_type=jnp.float32
    )
    context_rows = context_rows.reshape(ment_rows, local_cols).astype(jnp.bfloat16)
    attn_part = jnp.dot(context_rows, w_out, preferred_element_type=jnp.float32)
    local_block = gold_block - first_block
    owned = (local_block >= 0) & (local_block < own_blocks)
    safe_block = jnp.clip(local_block, 0, own_blocks - 1)
    flat_table = table.reshape(own_blocks * block_rows, width)
    picked = flat_table[safe_block * block_rows + gold_row]
    picked = jnp.where(owned[:, None], picked.astype(jnp.float32), 0.0)
    both = peer_sum(
        jnp.concatenate([attn_part.astype(jnp.bfloat16), picked.astype(jnp.bfloat16)], axis=0), 0
    )
    attn_out, gold_sum = both[:ment_rows], both[ment_rows:]
    golds = gold_sum.astype(jnp.bfloat16)
    resid = cls_rows.astype(jnp.float32) + attn_out
    centre = resid - jnp.mean(resid, axis=-1, keepdims=True)
    rstd = lax.rsqrt(jnp.mean(centre * centre, axis=-1, keepdims=True) + ln_eps)
    normed = centre * rstd
    embed = (normed * ln_gain + ln_bias).astype(jnp.bfloat16)
    inbatch = contract(embed, golds, 1, 1)
    negscore = contract(embed, flat_table, 1, 1)
    block_ids = first_block + jnp.arange(own_blocks, dtype=jnp.int32)
    listed = jnp.any(neg_blocks[0][:, None] == block_ids[None, :], axis=0).astype(jnp.float32)
    row_mask = jnp.repeat(listed, block_rows)
    neg_part = jnp.sum(jnp.exp(negscore) * row_mask[None, :], axis=1)
    neg_total = peer_sum(jnp.pad(neg_part.reshape(1, ment_rows), ((0, 7), (0, 0))), 1)[0]
    lse = jnp.log(jnp.sum(jnp.exp(inbatch), axis=1) + neg_total)
    eye = jnp.eye(ment_rows, dtype=jnp.float32)
    w_inb = (jnp.exp(inbatch - lse[:, None]) - eye).astype(jnp.bfloat16)
    w_neg = (jnp.exp(negscore - lse[:, None]) * row_mask[None, :]).astype(jnp.bfloat16)
    embed_part = jnp.dot(w_neg, flat_table, preferred_element_type=jnp.float32)
    d_embed = jnp.dot(w_inb, golds, preferred_element_type=jnp.float32) + peer_sum(
        embed_part.astype(jnp.bfloat16), 2
    )
    ln_terms = jnp.stack([jnp.sum(d_embed * normed, axis=0), jnp.sum(d_embed, axis=0)])
    upper = d_embed * ln_gain
    d_resid = rstd * (
        upper
        - jnp.mean(upper, axis=-1, keepdims=True)
        - normed * jnp.mean(upper * normed, axis=-1, keepdims=True)
    )
    d_resid_bf = d_resid.astype(jnp.bfloat16)
    d_context = contract(d_resid_bf, w_out, 1, 1).astype(jnp.bfloat16)
    context_head_gradient = d_context.reshape(ment_rows, local_heads, HD)
    probability_gradient = jnp.einsum(
        "ybn,yqbn->ybq", context_head_gradient, value_heads, preferred_element_type=jnp.float32
    )
    score_gradient = probs * (
        probability_gradient - jnp.sum(probs * probability_gradient, axis=-1, keepdims=True)
    )
    query_gradient = (
        jnp.einsum("qjp,qpjb->qjb", score_gradient, key_heads, preferred_element_type=jnp.float32)
        * score_scale
    )
    query_gradient = query_gradient.reshape(ment_rows, local_cols).astype(jnp.bfloat16)
    key_gradient = (
        jnp.einsum("ryk,ryo->rkyo", score_gradient, query_heads, preferred_element_type=jnp.float32)
        * score_scale
    )
    value_gradient = jnp.einsum(
        "ryk,ryo->rkyo", probability_half, context_head_gradient, preferred_element_type=jnp.float32
    )
    d_keyval = jnp.stack([key_gradient, value_gradient], axis=2).astype(jnp.bfloat16)
    kv_term = lax.dot_general(
        hidden_in, d_keyval, (((0, 1), (0, 1)), ((), ())), preferred_element_type=jnp.float32
    ).reshape(width, 2 * local_cols)
    query_term = contract(hidden_in[:, 0, :], query_gradient, 0, 0)
    share = ment_rows // lax.axis_size("ent")
    token_term = lax.dot_general(
        d_keyval,
        w_keyval.reshape(width, 2, local_heads, HD),
        (((2, 3, 4), (1, 2, 3)), ((), ())),
        preferred_element_type=jnp.float32,
    )
    resid_mine = lax.dynamic_slice_in_dim(d_resid, owner * share, share, 0)
    grad_hidden = peer_scatter(
        token_term.at[:, 0, :].add(contract(query_gradient, w_query, 1, 1)).astype(jnp.bfloat16),
        resid_mine,
        3,
    )
    gold_terms = contract(w_inb, embed, 0, 0)
    neg_weights = (
        w_neg.reshape(ment_rows, own_blocks, block_rows).transpose(0, 2, 1).reshape(ment_rows, -1)
    )
    slot = gold_row * own_blocks + safe_block
    hit = (slot[:, None] == jnp.arange(block_rows * own_blocks)[None, :]) & owned[:, None]
    gold_add = lax.dot_general(
        hit.astype(jnp.float32),
        gold_terms,
        (((0,), (0,)), ((), ())),
        precision=lax.Precision.HIGHEST,
        preferred_element_type=jnp.float32,
    )
    table_term = contract(neg_weights, embed, 0, 0) + gold_add
    parts = lax.axis_size("ment")
    qkv_rows = width // parts
    wo_cols = width // parts
    slab = own_blocks * width
    table_piece = table_term.reshape(parts, -1, own_blocks, width)
    rows_piece = jnp.concatenate(
        [query_term, kv_term, contract(d_resid_bf, context_rows, 0, 0)], axis=1
    ).reshape(parts, -1, own_blocks, width)
    ln_flat = ln_terms.T.reshape(parts, -1)
    ln_piece = jnp.pad(ln_flat, ((0, 0), (0, -ln_flat.shape[1] % slab))).reshape(
        parts, -1, own_blocks, width
    )
    pieces = [table_piece, rows_piece, ln_piece]
    counts = [piece.shape[1] for piece in pieces]
    merged = lax.psum_scatter(
        jnp.concatenate(pieces, axis=1).reshape(-1, own_blocks, width),
        "ment",
        scatter_dimension=0,
        tiled=True,
    )
    merged = lax.optimization_barrier(merged)
    table_sum = merged[: counts[0]]
    rows_sum = merged[counts[0] : counts[0] + counts[1]].reshape(qkv_rows, -1)
    ln_sum = merged[counts[0] + counts[1] :].reshape(-1)[: ln_flat.shape[1]]
    grad_table = table_sum.transpose(1, 0, 2)
    grad_qkv = rows_sum[:, : 3 * local_cols].reshape(qkv_rows, 3, local_cols)
    grad_wo = rows_sum[:, 3 * local_cols :].T
    grad_ln = ln_sum.reshape(wo_cols, 2).T
    return (grad_hidden, grad_qkv, grad_wo, grad_ln, grad_table)


def solution(mesh):
    placed = (
        P("ment", None, None),
        P(None, None, "ent"),
        P("ent", None),
        P(),
        P(),
        P("ent", None, None),
        P("ment"),
        P("ment"),
        P("ment"),
        P("ment", None),
    )
    return jax.shard_map(
        on_device,
        mesh=mesh,
        in_specs=placed,
        out_specs=(
            P(("ment", "ent"), None, None),
            P("ment", None, "ent"),
            P("ent", "ment"),
            P(None, "ment"),
            P("ent", "ment", None),
        ),
        check_vma=False,
    )
```

```python
import functools

import jax
import jax.numpy as jnp
from jax import lax
from jax.experimental import pallas as pl
from jax.experimental.pallas import tpu as pltpu
from jax.sharding import PartitionSpec as P

HD = 64
MESH = pl.DeviceIdType.MESH


def _greet_peers(row, me, n):
    barrier = pltpu.get_barrier_semaphore()
    for k in range(1, n):
        pl.semaphore_signal(
            barrier, inc=1, device_id=(row, lax.rem(me + k, n)), device_id_type=MESH
        )
    pl.semaphore_wait(barrier, n - 1)


def _peer_sum_kernel(n, x_ref, out_ref, recv, send_sem, recv_sem, own_sem):
    row = lax.axis_index("ment")
    me = lax.axis_index("ent")
    _greet_peers(row, me, n)
    sends = []
    for k in range(1, n):
        copy = pltpu.make_async_remote_copy(
            src_ref=x_ref,
            dst_ref=recv.at[me],
            send_sem=send_sem.at[k - 1],
            recv_sem=recv_sem.at[me],
            device_id=(row, lax.rem(me + k, n)),
            device_id_type=MESH,
        )
        copy.start()
        sends.append(copy)
    own = pltpu.make_async_copy(x_ref, recv.at[me], own_sem)
    own.start()
    for k in range(1, n):
        source = lax.rem(me + n - k, n)
        pltpu.make_async_remote_copy(
            src_ref=x_ref,
            dst_ref=recv.at[source],
            send_sem=send_sem.at[k - 1],
            recv_sem=recv_sem.at[source],
            device_id=(row, source),
            device_id_type=MESH,
        ).wait_recv()
    own.wait()
    for copy in sends:
        copy.wait_send()
    total = recv[0].astype(jnp.float32)
    for s in range(1, n):
        total = total + recv[s].astype(jnp.float32)
    out_ref[...] = total


def peer_sum(x, collective):
    n = lax.axis_size("ent")
    return pl.pallas_call(
        functools.partial(_peer_sum_kernel, n),
        out_shape=jax.ShapeDtypeStruct(x.shape, jnp.float32),
        in_specs=[pl.BlockSpec(memory_space=pltpu.VMEM)],
        out_specs=pl.BlockSpec(memory_space=pltpu.VMEM),
        scratch_shapes=[
            pltpu.VMEM((n,) + x.shape, x.dtype),
            pltpu.SemaphoreType.DMA((n - 1,)),
            pltpu.SemaphoreType.DMA((n,)),
            pltpu.SemaphoreType.DMA(()),
        ],
        compiler_params=pltpu.CompilerParams(collective_id=collective, has_side_effects=True),
    )(x)


def _peer_scatter_kernel(n, y_ref, out_ref, recv, send_sem, recv_sem, own_sem):
    row = lax.axis_index("ment")
    me = lax.axis_index("ent")
    share = out_ref.shape[0]
    _greet_peers(row, me, n)
    sends = []
    for k in range(1, n):
        target = lax.rem(me + k, n)
        copy = pltpu.make_async_remote_copy(
            src_ref=y_ref.at[pl.ds(target * share, share)],
            dst_ref=recv.at[me],
            send_sem=send_sem.at[k - 1],
            recv_sem=recv_sem.at[me],
            device_id=(row, target),
            device_id_type=MESH,
        )
        copy.start()
        sends.append(copy)
    own = pltpu.make_async_copy(y_ref.at[pl.ds(me * share, share)], recv.at[me], own_sem)
    own.start()
    for k in range(1, n):
        source = lax.rem(me + n - k, n)
        pltpu.make_async_remote_copy(
            src_ref=y_ref.at[pl.ds(0, share)],
            dst_ref=recv.at[source],
            send_sem=send_sem.at[k - 1],
            recv_sem=recv_sem.at[source],
            device_id=(row, source),
            device_id_type=MESH,
        ).wait_recv()
    own.wait()
    for copy in sends:
        copy.wait_send()
    def one_mention(i, carry):
        total = recv[0, i].astype(jnp.float32)
        for s in range(1, n):
            total = total + recv[s, i].astype(jnp.float32)
        out_ref[i] = total
        return carry

    lax.fori_loop(0, share, one_mention, 0)


def peer_scatter(y, collective):
    n = lax.axis_size("ent")
    share = y.shape[0] // n
    return pl.pallas_call(
        functools.partial(_peer_scatter_kernel, n),
        out_shape=jax.ShapeDtypeStruct((share,) + y.shape[1:], jnp.float32),
        in_specs=[pl.BlockSpec(memory_space=pltpu.VMEM)],
        out_specs=pl.BlockSpec(memory_space=pltpu.VMEM),
        scratch_shapes=[
            pltpu.VMEM((n, share) + y.shape[1:], y.dtype),
            pltpu.SemaphoreType.DMA((n - 1,)),
            pltpu.SemaphoreType.DMA((n,)),
            pltpu.SemaphoreType.DMA(()),
        ],
        compiler_params=pltpu.CompilerParams(collective_id=collective, has_side_effects=True),
    )(y)


ln_eps = 1e-06


def contract(left, right, left_dim, right_dim):
    return lax.dot_general(
        left, right, (((left_dim,), (right_dim,)), ((), ())), preferred_element_type=jnp.float32
    )


def on_device(
    hidden_in, w_qkv, w_out, ln_gain, ln_bias, table, key_len, gold_block, gold_row, neg_blocks
):
    ment_rows, seq_len, width = hidden_in.shape
    local_cols = w_qkv.shape[2]
    local_heads = local_cols // HD
    own_blocks, block_rows = (table.shape[0], table.shape[1])
    score_scale = HD ** (-0.5)
    owner = lax.axis_index("ent")
    first_block = owner * own_blocks
    cls_rows = hidden_in[:, 0, :]
    w_query = w_qkv[:, 0, :]
    w_keyval = w_qkv[:, 1:, :].reshape(width, 2 * local_cols)
    query = jnp.dot(cls_rows, w_query, preferred_element_type=jnp.float32).astype(jnp.bfloat16)
    keyval = lax.dot_general(
        hidden_in,
        w_keyval.reshape(width, 2, local_heads, HD),
        (((2,), (0,)), ((), ())),
        preferred_element_type=jnp.float32,
    ).astype(jnp.bfloat16)
    key_heads = keyval[:, :, 0]
    value_heads = keyval[:, :, 1]
    query_heads = query.reshape(ment_rows, local_heads, HD)
    attention_scores = (
        jnp.einsum("ybn,yqbn->ybq", query_heads, key_heads, preferred_element_type=jnp.float32)
        * score_scale
    )
    valid = (jnp.arange(seq_len, dtype=jnp.int32)[None, :] < key_len[:, None]).astype(jnp.float32)
    expo = jnp.exp(attention_scores) * valid[:, None, :]
    probs = expo / jnp.sum(expo, axis=-1, keepdims=True)
    probability_half = probs.astype(jnp.bfloat16)
    context_rows = jnp.einsum(
        "qjp,qpjb->qjb", probability_half, value_heads, preferred_element_type=jnp.float32
    )
    context_rows = context_rows.reshape(ment_rows, local_cols).astype(jnp.bfloat16)
    attn_part = jnp.dot(context_rows, w_out, preferred_element_type=jnp.float32)
    local_block = gold_block - first_block
    owned = (local_block >= 0) & (local_block < own_blocks)
    safe_block = jnp.clip(local_block, 0, own_blocks - 1)
    flat_table = table.reshape(own_blocks * block_rows, width)
    picked = flat_table[safe_block * block_rows + gold_row]
    picked = jnp.where(owned[:, None], picked.astype(jnp.float32), 0.0)
    both = peer_sum(
        jnp.concatenate([attn_part.astype(jnp.bfloat16), picked.astype(jnp.bfloat16)], axis=0), 0
    )
    attn_out, gold_sum = both[:ment_rows], both[ment_rows:]
    golds = gold_sum.astype(jnp.bfloat16)
    resid = cls_rows.astype(jnp.float32) + attn_out
    centre = resid - jnp.mean(resid, axis=-1, keepdims=True)
    rstd = lax.rsqrt(jnp.mean(centre * centre, axis=-1, keepdims=True) + ln_eps)
    normed = centre * rstd
    embed = (normed * ln_gain + ln_bias).astype(jnp.bfloat16)
    inbatch = contract(embed, golds, 1, 1)
    negscore = contract(embed, flat_table, 1, 1)
    block_ids = first_block + jnp.arange(own_blocks, dtype=jnp.int32)
    listed = jnp.any(neg_blocks[0][:, None] == block_ids[None, :], axis=0).astype(jnp.float32)
    row_mask = jnp.repeat(listed, block_rows)
    neg_part = jnp.sum(jnp.exp(negscore) * row_mask[None, :], axis=1)
    neg_total = peer_sum(jnp.pad(neg_part.reshape(1, ment_rows), ((0, 7), (0, 0))), 1)[0]
    lse = jnp.log(jnp.sum(jnp.exp(inbatch), axis=1) + neg_total)
    eye = jnp.eye(ment_rows, dtype=jnp.float32)
    w_inb = (jnp.exp(inbatch - lse[:, None]) - eye).astype(jnp.bfloat16)
    w_neg = (jnp.exp(negscore - lse[:, None]) * row_mask[None, :]).astype(jnp.bfloat16)
    embed_part = jnp.dot(w_neg, flat_table, preferred_element_type=jnp.float32)
    d_embed = jnp.dot(w_inb, golds, preferred_element_type=jnp.float32) + peer_sum(
        embed_part.astype(jnp.bfloat16), 2
    )
    ln_terms = jnp.stack([jnp.sum(d_embed * normed, axis=0), jnp.sum(d_embed, axis=0)])
    upper = d_embed * ln_gain
    d_resid = rstd * (
        upper
        - jnp.mean(upper, axis=-1, keepdims=True)
        - normed * jnp.mean(upper * normed, axis=-1, keepdims=True)
    )
    d_resid_bf = d_resid.astype(jnp.bfloat16)
    d_context = contract(d_resid_bf, w_out, 1, 1).astype(jnp.bfloat16)
    context_head_gradient = d_context.reshape(ment_rows, local_heads, HD)
    probability_gradient = jnp.einsum(
        "ybn,yqbn->ybq", context_head_gradient, value_heads, preferred_element_type=jnp.float32
    )
    score_gradient = probs * (
        probability_gradient - jnp.sum(probs * probability_gradient, axis=-1, keepdims=True)
    )
    query_gradient = (
        jnp.einsum("qjp,qpjb->qjb", score_gradient, key_heads, preferred_element_type=jnp.float32)
        * score_scale
    )
    query_gradient = query_gradient.reshape(ment_rows, local_cols).astype(jnp.bfloat16)
    key_gradient = (
        jnp.einsum("ryk,ryo->rkyo", score_gradient, query_heads, preferred_element_type=jnp.float32)
        * score_scale
    )
    value_gradient = jnp.einsum(
        "ryk,ryo->rkyo", probability_half, context_head_gradient, preferred_element_type=jnp.float32
    )
    d_keyval = jnp.stack([key_gradient, value_gradient], axis=2).astype(jnp.bfloat16)
    kv_term = lax.dot_general(
        hidden_in, d_keyval, (((0, 1), (0, 1)), ((), ())), preferred_element_type=jnp.float32
    ).reshape(width, 2 * local_cols)
    query_term = contract(hidden_in[:, 0, :], query_gradient, 0, 0)
    share = ment_rows // lax.axis_size("ent")
    token_term = lax.dot_general(
        d_keyval,
        w_keyval.reshape(width, 2, local_heads, HD),
        (((2, 3, 4), (1, 2, 3)), ((), ())),
        preferred_element_type=jnp.float32,
    )
    resid_mine = lax.dynamic_slice_in_dim(d_resid, owner * share, share, 0)
    summed = peer_scatter(
        token_term.at[:, 0, :].add(contract(query_gradient, w_query, 1, 1)).astype(jnp.bfloat16),
        3,
    )
    grad_hidden = summed.at[:, 0, :].add(resid_mine).astype(jnp.bfloat16)
    gold_terms = contract(w_inb, embed, 0, 0)
    neg_weights = (
        w_neg.reshape(ment_rows, own_blocks, block_rows).transpose(0, 2, 1).reshape(ment_rows, -1)
    )
    slot = gold_row * own_blocks + safe_block
    hit = (slot[:, None] == jnp.arange(block_rows * own_blocks)[None, :]) & owned[:, None]
    gold_add = lax.dot_general(
        hit.astype(jnp.float32),
        gold_terms,
        (((0,), (0,)), ((), ())),
        precision=lax.Precision.HIGHEST,
        preferred_element_type=jnp.float32,
    )
    table_term = contract(neg_weights, embed, 0, 0) + gold_add
    parts = lax.axis_size("ment")
    qkv_rows = width // parts
    wo_cols = width // parts
    slab = own_blocks * width
    table_piece = table_term.reshape(parts, -1, own_blocks, width)
    rows_piece = jnp.concatenate(
        [query_term, kv_term, contract(d_resid_bf, context_rows, 0, 0)], axis=1
    ).reshape(parts, -1, own_blocks, width)
    ln_flat = ln_terms.T.reshape(parts, -1)
    ln_piece = jnp.pad(ln_flat, ((0, 0), (0, -ln_flat.shape[1] % slab))).reshape(
        parts, -1, own_blocks, width
    )
    pieces = [table_piece, rows_piece, ln_piece]
    counts = [piece.shape[1] for piece in pieces]
    merged = lax.psum_scatter(
        jnp.concatenate(pieces, axis=1).reshape(-1, own_blocks, width),
        "ment",
        scatter_dimension=0,
        tiled=True,
    )
    merged = lax.optimization_barrier(merged)
    table_sum = merged[: counts[0]]
    rows_sum = merged[counts[0] : counts[0] + counts[1]].reshape(qkv_rows, -1)
    ln_sum = merged[counts[0] + counts[1], 0, : ln_flat.shape[1]]
    grad_table = table_sum.transpose(1, 0, 2)
    grad_qkv = rows_sum[:, : 3 * local_cols].reshape(qkv_rows, 3, local_cols)
    grad_wo = rows_sum[:, 3 * local_cols :].T
    grad_ln = ln_sum.reshape(wo_cols, 2).T
    return (grad_hidden, grad_qkv, grad_wo, grad_ln, grad_table)


def solution(mesh):
    placed = (
        P("ment", None, None),
        P(None, None, "ent"),
        P("ent", None),
        P(),
        P(),
        P("ent", None, None),
        P("ment"),
        P("ment"),
        P("ment"),
        P("ment", None),
    )
    return jax.shard_map(
        on_device,
        mesh=mesh,
        in_specs=placed,
        out_specs=(
            P(("ment", "ent"), None, None),
            P("ment", None, "ent"),
            P("ent", "ment"),
            P(None, "ment"),
            P("ent", "ment", None),
        ),
        check_vma=False,
    )
```

```python
import functools

import jax
import jax.numpy as jnp
from jax import lax
from jax.experimental import pallas as pl
from jax.experimental.pallas import tpu as pltpu
from jax.sharding import PartitionSpec as P

HD = 64
MESH = pl.DeviceIdType.MESH


def _greet_peers(row, me, n):
    barrier = pltpu.get_barrier_semaphore()
    for k in range(1, n):
        pl.semaphore_signal(
            barrier, inc=1, device_id=(row, lax.rem(me + k, n)), device_id_type=MESH
        )
    pl.semaphore_wait(barrier, n - 1)


def _peer_sum_kernel(n, x_ref, out_ref, recv, send_sem, recv_sem, own_sem):
    row = lax.axis_index("ment")
    me = lax.axis_index("ent")
    _greet_peers(row, me, n)
    sends = []
    for k in range(1, n):
        copy = pltpu.make_async_remote_copy(
            src_ref=x_ref,
            dst_ref=recv.at[me],
            send_sem=send_sem.at[k - 1],
            recv_sem=recv_sem.at[me],
            device_id=(row, lax.rem(me + k, n)),
            device_id_type=MESH,
        )
        copy.start()
        sends.append(copy)
    own = pltpu.make_async_copy(x_ref, recv.at[me], own_sem)
    own.start()
    for k in range(1, n):
        source = lax.rem(me + n - k, n)
        pltpu.make_async_remote_copy(
            src_ref=x_ref,
            dst_ref=recv.at[source],
            send_sem=send_sem.at[k - 1],
            recv_sem=recv_sem.at[source],
            device_id=(row, source),
            device_id_type=MESH,
        ).wait_recv()
    own.wait()
    for copy in sends:
        copy.wait_send()
    total = recv[0].astype(jnp.float32)
    for s in range(1, n):
        total = total + recv[s].astype(jnp.float32)
    out_ref[...] = total


def peer_sum(x, collective):
    n = lax.axis_size("ent")
    return pl.pallas_call(
        functools.partial(_peer_sum_kernel, n),
        out_shape=jax.ShapeDtypeStruct(x.shape, jnp.float32),
        in_specs=[pl.BlockSpec(memory_space=pltpu.VMEM)],
        out_specs=pl.BlockSpec(memory_space=pltpu.VMEM),
        scratch_shapes=[
            pltpu.VMEM((n,) + x.shape, x.dtype),
            pltpu.SemaphoreType.DMA((n - 1,)),
            pltpu.SemaphoreType.DMA((n,)),
            pltpu.SemaphoreType.DMA(()),
        ],
        compiler_params=pltpu.CompilerParams(collective_id=collective, has_side_effects=True),
    )(x)


def _peer_scatter_kernel(n, y_ref, out_ref, recv, send_sem, recv_sem, own_sem):
    row = lax.axis_index("ment")
    me = lax.axis_index("ent")
    share = out_ref.shape[0]
    _greet_peers(row, me, n)
    sends = []
    for k in range(1, n):
        target = lax.rem(me + k, n)
        copy = pltpu.make_async_remote_copy(
            src_ref=y_ref.at[pl.ds(target * share, share)],
            dst_ref=recv.at[me],
            send_sem=send_sem.at[k - 1],
            recv_sem=recv_sem.at[me],
            device_id=(row, target),
            device_id_type=MESH,
        )
        copy.start()
        sends.append(copy)
    own = pltpu.make_async_copy(y_ref.at[pl.ds(me * share, share)], recv.at[me], own_sem)
    own.start()
    for k in range(1, n):
        source = lax.rem(me + n - k, n)
        pltpu.make_async_remote_copy(
            src_ref=y_ref.at[pl.ds(0, share)],
            dst_ref=recv.at[source],
            send_sem=send_sem.at[k - 1],
            recv_sem=recv_sem.at[source],
            device_id=(row, source),
            device_id_type=MESH,
        ).wait_recv()
    own.wait()
    for copy in sends:
        copy.wait_send()
    def one_mention(i, carry):
        total = recv[0, i].astype(jnp.float32)
        for s in range(1, n):
            total = total + recv[s, i].astype(jnp.float32)
        out_ref[i] = total
        return carry

    lax.fori_loop(0, share, one_mention, 0)


def peer_scatter(y, collective):
    n = lax.axis_size("ent")
    share = y.shape[0] // n
    return pl.pallas_call(
        functools.partial(_peer_scatter_kernel, n),
        out_shape=jax.ShapeDtypeStruct((share,) + y.shape[1:], jnp.float32),
        in_specs=[pl.BlockSpec(memory_space=pltpu.VMEM)],
        out_specs=pl.BlockSpec(memory_space=pltpu.VMEM),
        scratch_shapes=[
            pltpu.VMEM((n, share) + y.shape[1:], y.dtype),
            pltpu.SemaphoreType.DMA((n - 1,)),
            pltpu.SemaphoreType.DMA((n,)),
            pltpu.SemaphoreType.DMA(()),
        ],
        compiler_params=pltpu.CompilerParams(collective_id=collective, has_side_effects=True),
    )(y)


ln_eps = 1e-06


def contract(left, right, left_dim, right_dim):
    return lax.dot_general(
        left, right, (((left_dim,), (right_dim,)), ((), ())), preferred_element_type=jnp.float32
    )


def on_device(
    hidden_in, w_qkv, w_out, ln_gain, ln_bias, table, key_len, gold_block, gold_row, neg_blocks
):
    ment_rows, seq_len, width = hidden_in.shape
    local_cols = w_qkv.shape[2]
    local_heads = local_cols // HD
    own_blocks, block_rows = (table.shape[0], table.shape[1])
    score_scale = HD ** (-0.5)
    owner = lax.axis_index("ent")
    first_block = owner * own_blocks
    cls_rows = hidden_in[:, 0, :]
    w_query = w_qkv[:, 0, :]
    w_keyval = w_qkv[:, 1:, :].reshape(width, 2 * local_cols)
    query = jnp.dot(cls_rows, w_query, preferred_element_type=jnp.float32).astype(jnp.bfloat16)
    keyval = lax.dot_general(
        hidden_in,
        w_keyval.reshape(width, 2, local_heads, HD),
        (((2,), (0,)), ((), ())),
        preferred_element_type=jnp.float32,
    ).astype(jnp.bfloat16)
    key_heads = keyval[:, :, 0]
    value_heads = keyval[:, :, 1]
    query_heads = query.reshape(ment_rows, local_heads, HD)
    attention_scores = (
        jnp.einsum("ybn,yqbn->ybq", query_heads, key_heads, preferred_element_type=jnp.float32)
        * score_scale
    )
    valid = (jnp.arange(seq_len, dtype=jnp.int32)[None, :] < key_len[:, None]).astype(jnp.float32)
    expo = jnp.exp(attention_scores) * valid[:, None, :]
    probs = expo / jnp.sum(expo, axis=-1, keepdims=True)
    probability_half = probs.astype(jnp.bfloat16)
    context_rows = jnp.einsum(
        "qjp,qpjb->qjb", probability_half, value_heads, preferred_element_type=jnp.float32
    )
    context_rows = context_rows.reshape(ment_rows, local_cols).astype(jnp.bfloat16)
    attn_part = jnp.dot(context_rows, w_out, preferred_element_type=jnp.float32)
    local_block = gold_block - first_block
    owned = (local_block >= 0) & (local_block < own_blocks)
    safe_block = jnp.clip(local_block, 0, own_blocks - 1)
    flat_table = table.reshape(own_blocks * block_rows, width)
    picked = flat_table[safe_block * block_rows + gold_row]
    picked = jnp.where(owned[:, None], picked.astype(jnp.float32), 0.0)
    both = peer_sum(
        jnp.concatenate([attn_part.astype(jnp.bfloat16), picked.astype(jnp.bfloat16)], axis=0), 0
    )
    attn_out, gold_sum = both[:ment_rows], both[ment_rows:]
    golds = gold_sum.astype(jnp.bfloat16)
    resid = cls_rows.astype(jnp.float32) + attn_out
    centre = resid - jnp.mean(resid, axis=-1, keepdims=True)
    rstd = lax.rsqrt(jnp.mean(centre * centre, axis=-1, keepdims=True) + ln_eps)
    normed = centre * rstd
    embed = (normed * ln_gain + ln_bias).astype(jnp.bfloat16)
    inbatch = contract(embed, golds, 1, 1)
    negscore = contract(embed, flat_table, 1, 1)
    block_ids = first_block + jnp.arange(own_blocks, dtype=jnp.int32)
    listed = jnp.any(neg_blocks[0][:, None] == block_ids[None, :], axis=0).astype(jnp.float32)
    row_mask = jnp.repeat(listed, block_rows)
    neg_part = jnp.sum(jnp.exp(negscore) * row_mask[None, :], axis=1)
    neg_total = peer_sum(jnp.pad(neg_part.reshape(1, ment_rows), ((0, 7), (0, 0))), 1)[0]
    lse = jnp.log(jnp.sum(jnp.exp(inbatch), axis=1) + neg_total)
    eye = jnp.eye(ment_rows, dtype=jnp.float32)
    w_inb = (jnp.exp(inbatch - lse[:, None]) - eye).astype(jnp.bfloat16)
    w_neg = (jnp.exp(negscore - lse[:, None]) * row_mask[None, :]).astype(jnp.bfloat16)
    embed_part = jnp.dot(w_neg, flat_table, preferred_element_type=jnp.float32)
    d_embed = jnp.dot(w_inb, golds, preferred_element_type=jnp.float32) + peer_sum(
        embed_part.astype(jnp.bfloat16), 2
    )
    ln_terms = jnp.stack([jnp.sum(d_embed * normed, axis=0), jnp.sum(d_embed, axis=0)])
    upper = d_embed * ln_gain
    d_resid = rstd * (
        upper
        - jnp.mean(upper, axis=-1, keepdims=True)
        - normed * jnp.mean(upper * normed, axis=-1, keepdims=True)
    )
    d_resid_bf = d_resid.astype(jnp.bfloat16)
    d_context = contract(d_resid_bf, w_out, 1, 1).astype(jnp.bfloat16)
    context_head_gradient = d_context.reshape(ment_rows, local_heads, HD)
    probability_gradient = jnp.einsum(
        "ybn,yqbn->ybq", context_head_gradient, value_heads, preferred_element_type=jnp.float32
    )
    score_gradient = probs * (
        probability_gradient - jnp.sum(probs * probability_gradient, axis=-1, keepdims=True)
    )
    query_gradient = (
        jnp.einsum("qjp,qpjb->qjb", score_gradient, key_heads, preferred_element_type=jnp.float32)
        * score_scale
    )
    query_gradient = query_gradient.reshape(ment_rows, local_cols).astype(jnp.bfloat16)
    key_gradient = (
        jnp.einsum("ryk,ryo->rkyo", score_gradient, query_heads, preferred_element_type=jnp.float32)
        * score_scale
    )
    value_gradient = jnp.einsum(
        "ryk,ryo->rkyo", probability_half, context_head_gradient, preferred_element_type=jnp.float32
    )
    d_keyval = jnp.stack([key_gradient, value_gradient], axis=2).astype(jnp.bfloat16)
    kv_term = lax.dot_general(
        d_keyval, hidden_in, (((0, 1), (0, 1)), ((), ())), preferred_element_type=jnp.float32
    ).reshape(2 * local_cols, width).T
    query_term = contract(hidden_in[:, 0, :], query_gradient, 0, 0)
    share = ment_rows // lax.axis_size("ent")
    token_term = lax.dot_general(
        d_keyval,
        w_keyval.reshape(width, 2, local_heads, HD),
        (((2, 3, 4), (1, 2, 3)), ((), ())),
        preferred_element_type=jnp.float32,
    )
    resid_mine = lax.dynamic_slice_in_dim(d_resid, owner * share, share, 0)
    summed = peer_scatter(
        token_term.at[:, 0, :].add(contract(query_gradient, w_query, 1, 1)).astype(jnp.bfloat16),
        3,
    )
    grad_hidden = summed.at[:, 0, :].add(resid_mine).astype(jnp.bfloat16)
    gold_terms = contract(w_inb, embed, 0, 0)
    neg_weights = (
        w_neg.reshape(ment_rows, own_blocks, block_rows).transpose(0, 2, 1).reshape(ment_rows, -1)
    )
    slot = gold_row * own_blocks + safe_block
    hit = (slot[:, None] == jnp.arange(block_rows * own_blocks)[None, :]) & owned[:, None]
    gold_add = lax.dot_general(
        hit.astype(jnp.float32),
        gold_terms,
        (((0,), (0,)), ((), ())),
        precision=lax.Precision.HIGHEST,
        preferred_element_type=jnp.float32,
    )
    table_term = contract(neg_weights, embed, 0, 0) + gold_add
    parts = lax.axis_size("ment")
    qkv_rows = width // parts
    wo_cols = width // parts
    slab = own_blocks * width
    table_piece = table_term.reshape(parts, -1, own_blocks, width)
    rows_piece = jnp.concatenate(
        [query_term, kv_term, contract(d_resid_bf, context_rows, 0, 0)], axis=1
    ).reshape(parts, -1, own_blocks, width)
    ln_flat = ln_terms.T.reshape(parts, -1)
    ln_piece = jnp.pad(ln_flat, ((0, 0), (0, -ln_flat.shape[1] % slab))).reshape(
        parts, -1, own_blocks, width
    )
    pieces = [table_piece, rows_piece, ln_piece]
    counts = [piece.shape[1] for piece in pieces]
    merged = lax.psum_scatter(
        jnp.concatenate(pieces, axis=1).reshape(-1, own_blocks, width),
        "ment",
        scatter_dimension=0,
        tiled=True,
    )
    merged = lax.optimization_barrier(merged)
    table_sum = merged[: counts[0]]
    rows_sum = merged[counts[0] : counts[0] + counts[1]].reshape(qkv_rows, -1)
    ln_sum = merged[counts[0] + counts[1], 0, : ln_flat.shape[1]]
    grad_table = table_sum.transpose(1, 0, 2)
    grad_qkv = rows_sum[:, : 3 * local_cols].reshape(qkv_rows, 3, local_cols)
    grad_wo = rows_sum[:, 3 * local_cols :].T
    grad_ln = ln_sum.reshape(wo_cols, 2).T
    return (grad_hidden, grad_qkv, grad_wo, grad_ln, grad_table)


def solution(mesh):
    placed = (
        P("ment", None, None),
        P(None, None, "ent"),
        P("ent", None),
        P(),
        P(),
        P("ent", None, None),
        P("ment"),
        P("ment"),
        P("ment"),
        P("ment", None),
    )
    return jax.shard_map(
        on_device,
        mesh=mesh,
        in_specs=placed,
        out_specs=(
            P(("ment", "ent"), None, None),
            P("ment", None, "ent"),
            P("ent", "ment"),
            P(None, "ment"),
            P("ent", "ment", None),
        ),
        check_vma=False,
    )
```

```python
import functools

import jax
import jax.numpy as jnp
from jax import lax
from jax.experimental import pallas as pl
from jax.experimental.pallas import tpu as pltpu
from jax.sharding import PartitionSpec as P

HD = 64
MESH = pl.DeviceIdType.MESH


def _greet_peers(row, me, n):
    barrier = pltpu.get_barrier_semaphore()
    for k in range(1, n):
        pl.semaphore_signal(
            barrier, inc=1, device_id=(row, lax.rem(me + k, n)), device_id_type=MESH
        )
    pl.semaphore_wait(barrier, n - 1)


def _peer_sum_kernel(n, x_ref, out_ref, recv, send_sem, recv_sem, own_sem):
    row = lax.axis_index("ment")
    me = lax.axis_index("ent")
    _greet_peers(row, me, n)
    sends = []
    for k in range(1, n):
        copy = pltpu.make_async_remote_copy(
            src_ref=x_ref,
            dst_ref=recv.at[me],
            send_sem=send_sem.at[k - 1],
            recv_sem=recv_sem.at[me],
            device_id=(row, lax.rem(me + k, n)),
            device_id_type=MESH,
        )
        copy.start()
        sends.append(copy)
    own = pltpu.make_async_copy(x_ref, recv.at[me], own_sem)
    own.start()
    for k in range(1, n):
        source = lax.rem(me + n - k, n)
        pltpu.make_async_remote_copy(
            src_ref=x_ref,
            dst_ref=recv.at[source],
            send_sem=send_sem.at[k - 1],
            recv_sem=recv_sem.at[source],
            device_id=(row, source),
            device_id_type=MESH,
        ).wait_recv()
    own.wait()
    for copy in sends:
        copy.wait_send()
    total = recv[0].astype(jnp.float32)
    for s in range(1, n):
        total = total + recv[s].astype(jnp.float32)
    out_ref[...] = total


def peer_sum(x, collective):
    n = lax.axis_size("ent")
    return pl.pallas_call(
        functools.partial(_peer_sum_kernel, n),
        out_shape=jax.ShapeDtypeStruct(x.shape, jnp.float32),
        in_specs=[pl.BlockSpec(memory_space=pltpu.VMEM)],
        out_specs=pl.BlockSpec(memory_space=pltpu.VMEM),
        scratch_shapes=[
            pltpu.VMEM((n,) + x.shape, x.dtype),
            pltpu.SemaphoreType.DMA((n - 1,)),
            pltpu.SemaphoreType.DMA((n,)),
            pltpu.SemaphoreType.DMA(()),
        ],
        compiler_params=pltpu.CompilerParams(collective_id=collective, has_side_effects=True),
    )(x)


def _peer_scatter_kernel(n, y_ref, out_ref, recv, send_sem, recv_sem, own_sem):
    row = lax.axis_index("ment")
    me = lax.axis_index("ent")
    share = out_ref.shape[0]
    _greet_peers(row, me, n)
    sends = []
    for k in range(1, n):
        target = lax.rem(me + k, n)
        copy = pltpu.make_async_remote_copy(
            src_ref=y_ref.at[pl.ds(target * share, share)],
            dst_ref=recv.at[me],
            send_sem=send_sem.at[k - 1],
            recv_sem=recv_sem.at[me],
            device_id=(row, target),
            device_id_type=MESH,
        )
        copy.start()
        sends.append(copy)
    own = pltpu.make_async_copy(y_ref.at[pl.ds(me * share, share)], recv.at[me], own_sem)
    own.start()
    for k in range(1, n):
        source = lax.rem(me + n - k, n)
        pltpu.make_async_remote_copy(
            src_ref=y_ref.at[pl.ds(0, share)],
            dst_ref=recv.at[source],
            send_sem=send_sem.at[k - 1],
            recv_sem=recv_sem.at[source],
            device_id=(row, source),
            device_id_type=MESH,
        ).wait_recv()
    own.wait()
    for copy in sends:
        copy.wait_send()
    def one_mention(i, carry):
        total = recv[0, i].astype(jnp.float32)
        for s in range(1, n):
            total = total + recv[s, i].astype(jnp.float32)
        out_ref[i] = total
        return carry

    lax.fori_loop(0, share, one_mention, 0)


def peer_scatter(y, collective):
    n = lax.axis_size("ent")
    share = y.shape[0] // n
    return pl.pallas_call(
        functools.partial(_peer_scatter_kernel, n),
        out_shape=jax.ShapeDtypeStruct((share,) + y.shape[1:], jnp.float32),
        in_specs=[pl.BlockSpec(memory_space=pltpu.VMEM)],
        out_specs=pl.BlockSpec(memory_space=pltpu.VMEM),
        scratch_shapes=[
            pltpu.VMEM((n, share) + y.shape[1:], y.dtype),
            pltpu.SemaphoreType.DMA((n - 1,)),
            pltpu.SemaphoreType.DMA((n,)),
            pltpu.SemaphoreType.DMA(()),
        ],
        compiler_params=pltpu.CompilerParams(collective_id=collective, has_side_effects=True),
    )(y)


ln_eps = 1e-06


def contract(left, right, left_dim, right_dim):
    return lax.dot_general(
        left, right, (((left_dim,), (right_dim,)), ((), ())), preferred_element_type=jnp.float32
    )


def on_device(
    hidden_in, w_qkv, w_out, ln_gain, ln_bias, table, key_len, gold_block, gold_row, neg_blocks
):
    ment_rows, seq_len, width = hidden_in.shape
    local_cols = w_qkv.shape[2]
    local_heads = local_cols // HD
    own_blocks, block_rows = (table.shape[0], table.shape[1])
    score_scale = HD ** (-0.5)
    owner = lax.axis_index("ent")
    first_block = owner * own_blocks
    cls_rows = hidden_in[:, 0, :]
    w_query = w_qkv[:, 0, :]
    w_keyval = w_qkv[:, 1:, :].reshape(width, 2 * local_cols)
    query = jnp.dot(cls_rows, w_query, preferred_element_type=jnp.float32).astype(jnp.bfloat16)
    keyval = lax.dot_general(
        hidden_in,
        w_keyval.reshape(width, 2, local_heads, HD),
        (((2,), (0,)), ((), ())),
        preferred_element_type=jnp.float32,
    ).astype(jnp.bfloat16)
    key_heads = keyval[:, :, 0]
    value_heads = keyval[:, :, 1]
    query_heads = query.reshape(ment_rows, local_heads, HD)
    attention_scores = (
        jnp.einsum("ybn,yqbn->ybq", query_heads, key_heads, preferred_element_type=jnp.float32)
        * score_scale
    )
    valid = (jnp.arange(seq_len, dtype=jnp.int32)[None, :] < key_len[:, None]).astype(jnp.float32)
    expo = jnp.exp(attention_scores) * valid[:, None, :]
    probs = expo / jnp.sum(expo, axis=-1, keepdims=True)
    probability_half = probs.astype(jnp.bfloat16)
    context_rows = jnp.einsum(
        "qjp,qpjb->qjb", probability_half, value_heads, preferred_element_type=jnp.float32
    )
    context_rows = context_rows.reshape(ment_rows, local_cols).astype(jnp.bfloat16)
    attn_part = jnp.dot(context_rows, w_out, preferred_element_type=jnp.float32)
    local_block = gold_block - first_block
    owned = (local_block >= 0) & (local_block < own_blocks)
    safe_block = jnp.clip(local_block, 0, own_blocks - 1)
    flat_table = table.reshape(own_blocks * block_rows, width)
    picked_row = safe_block * block_rows + gold_row
    pick = (picked_row[:, None] == jnp.arange(own_blocks * block_rows)[None, :]).astype(table.dtype)
    picked = jnp.dot(pick, flat_table, preferred_element_type=jnp.float32)
    picked = jnp.where(owned[:, None], picked.astype(jnp.float32), 0.0)
    both = peer_sum(
        jnp.concatenate([attn_part.astype(jnp.bfloat16), picked.astype(jnp.bfloat16)], axis=0), 0
    )
    attn_out, gold_sum = both[:ment_rows], both[ment_rows:]
    golds = gold_sum.astype(jnp.bfloat16)
    resid = cls_rows.astype(jnp.float32) + attn_out
    centre = resid - jnp.mean(resid, axis=-1, keepdims=True)
    rstd = lax.rsqrt(jnp.mean(centre * centre, axis=-1, keepdims=True) + ln_eps)
    normed = centre * rstd
    embed = (normed * ln_gain + ln_bias).astype(jnp.bfloat16)
    inbatch = contract(embed, golds, 1, 1)
    negscore = contract(embed, flat_table, 1, 1)
    block_ids = first_block + jnp.arange(own_blocks, dtype=jnp.int32)
    listed = jnp.any(neg_blocks[0][:, None] == block_ids[None, :], axis=0).astype(jnp.float32)
    row_mask = jnp.repeat(listed, block_rows)
    neg_part = jnp.sum(jnp.exp(negscore) * row_mask[None, :], axis=1)
    neg_total = peer_sum(jnp.pad(neg_part.reshape(1, ment_rows), ((0, 7), (0, 0))), 1)[0]
    lse = jnp.log(jnp.sum(jnp.exp(inbatch), axis=1) + neg_total)
    eye = jnp.eye(ment_rows, dtype=jnp.float32)
    w_inb = (jnp.exp(inbatch - lse[:, None]) - eye).astype(jnp.bfloat16)
    w_neg = (jnp.exp(negscore - lse[:, None]) * row_mask[None, :]).astype(jnp.bfloat16)
    embed_part = jnp.dot(w_neg, flat_table, preferred_element_type=jnp.float32)
    d_embed = jnp.dot(w_inb, golds, preferred_element_type=jnp.float32) + peer_sum(
        embed_part.astype(jnp.bfloat16), 2
    )
    ln_terms = jnp.stack([jnp.sum(d_embed * normed, axis=0), jnp.sum(d_embed, axis=0)])
    upper = d_embed * ln_gain
    d_resid = rstd * (
        upper
        - jnp.mean(upper, axis=-1, keepdims=True)
        - normed * jnp.mean(upper * normed, axis=-1, keepdims=True)
    )
    d_resid_bf = d_resid.astype(jnp.bfloat16)
    d_context = contract(d_resid_bf, w_out, 1, 1).astype(jnp.bfloat16)
    context_head_gradient = d_context.reshape(ment_rows, local_heads, HD)
    probability_gradient = jnp.einsum(
        "ybn,yqbn->ybq", context_head_gradient, value_heads, preferred_element_type=jnp.float32
    )
    score_gradient = probs * (
        probability_gradient - jnp.sum(probs * probability_gradient, axis=-1, keepdims=True)
    )
    query_gradient = (
        jnp.einsum("qjp,qpjb->qjb", score_gradient, key_heads, preferred_element_type=jnp.float32)
        * score_scale
    )
    query_gradient = query_gradient.reshape(ment_rows, local_cols).astype(jnp.bfloat16)
    key_gradient = (
        jnp.einsum("ryk,ryo->rkyo", score_gradient, query_heads, preferred_element_type=jnp.float32)
        * score_scale
    )
    value_gradient = jnp.einsum(
        "ryk,ryo->rkyo", probability_half, context_head_gradient, preferred_element_type=jnp.float32
    )
    d_keyval = jnp.stack([key_gradient, value_gradient], axis=2).astype(jnp.bfloat16)
    kv_term = lax.dot_general(
        d_keyval, hidden_in, (((0, 1), (0, 1)), ((), ())), preferred_element_type=jnp.float32
    ).reshape(2 * local_cols, width).T
    query_term = contract(hidden_in[:, 0, :], query_gradient, 0, 0)
    share = ment_rows // lax.axis_size("ent")
    token_term = lax.dot_general(
        d_keyval,
        w_keyval.reshape(width, 2, local_heads, HD),
        (((2, 3, 4), (1, 2, 3)), ((), ())),
        preferred_element_type=jnp.float32,
    )
    resid_mine = lax.dynamic_slice_in_dim(d_resid, owner * share, share, 0)
    summed = peer_scatter(
        token_term.at[:, 0, :].add(contract(query_gradient, w_query, 1, 1)).astype(jnp.bfloat16),
        3,
    )
    grad_hidden = summed.at[:, 0, :].add(resid_mine).astype(jnp.bfloat16)
    gold_terms = contract(w_inb, embed, 0, 0)
    neg_weights = (
        w_neg.reshape(ment_rows, own_blocks, block_rows).transpose(0, 2, 1).reshape(ment_rows, -1)
    )
    slot = gold_row * own_blocks + safe_block
    hit = (slot[:, None] == jnp.arange(block_rows * own_blocks)[None, :]) & owned[:, None]
    gold_add = lax.dot_general(
        hit.astype(jnp.float32),
        gold_terms,
        (((0,), (0,)), ((), ())),
        precision=lax.Precision.HIGHEST,
        preferred_element_type=jnp.float32,
    )
    table_term = contract(neg_weights, embed, 0, 0) + gold_add
    parts = lax.axis_size("ment")
    qkv_rows = width // parts
    wo_cols = width // parts
    slab = own_blocks * width
    table_piece = table_term.reshape(parts, -1, own_blocks, width)
    rows_piece = jnp.concatenate(
        [query_term, kv_term, contract(d_resid_bf, context_rows, 0, 0)], axis=1
    ).reshape(parts, -1, own_blocks, width)
    ln_flat = ln_terms.T.reshape(parts, -1)
    ln_piece = jnp.pad(ln_flat, ((0, 0), (0, -ln_flat.shape[1] % slab))).reshape(
        parts, -1, own_blocks, width
    )
    pieces = [table_piece, rows_piece, ln_piece]
    counts = [piece.shape[1] for piece in pieces]
    merged = lax.psum_scatter(
        jnp.concatenate(pieces, axis=1).reshape(-1, own_blocks, width),
        "ment",
        scatter_dimension=0,
        tiled=True,
    )
    merged = lax.optimization_barrier(merged)
    table_sum = merged[: counts[0]]
    rows_sum = merged[counts[0] : counts[0] + counts[1]].reshape(qkv_rows, -1)
    ln_sum = merged[counts[0] + counts[1], 0, : ln_flat.shape[1]]
    grad_table = table_sum.transpose(1, 0, 2)
    grad_qkv = rows_sum[:, : 3 * local_cols].reshape(qkv_rows, 3, local_cols)
    grad_wo = rows_sum[:, 3 * local_cols :].T
    grad_ln = ln_sum.reshape(wo_cols, 2).T
    return (grad_hidden, grad_qkv, grad_wo, grad_ln, grad_table)


def solution(mesh):
    placed = (
        P("ment", None, None),
        P(None, None, "ent"),
        P("ent", None),
        P(),
        P(),
        P("ent", None, None),
        P("ment"),
        P("ment"),
        P("ment"),
        P("ment", None),
    )
    return jax.shard_map(
        on_device,
        mesh=mesh,
        in_specs=placed,
        out_specs=(
            P(("ment", "ent"), None, None),
            P("ment", None, "ent"),
            P("ent", "ment"),
            P(None, "ment"),
            P("ent", "ment", None),
        ),
        check_vma=False,
    )
```
